1024 devices in a mesh: ctx: 64 (over z, x_lo), tp: 16 (over y, x_hi, core).
Axes of the slice: x: 4 (x_hi: 2, x_lo: 2; x = x_hi * 2 + x_lo), y: 4, z: 32, core: 2. Of those that a mesh axis runs over, the one named last changes fastest.
Arguments:
- queries: bfloat16 [16384, 8192], P('ctx', 'tp'), may hold values from -6 to 6
- keys: bfloat16 [16384, 2048], P('ctx', 'tp'), may hold values from -6 to 6
- values: bfloat16 [16384, 2048], P('ctx', 'tp'), may hold values from -6 to 6
- outputs: bfloat16 [16384, 8192], P('ctx', 'tp'), may hold values from -6 to 6
- out_grad: bfloat16 [16384, 8192], P('ctx', 'tp'), may hold values from -6 to 6
- log_norm: float32 [16384, 64], P('ctx', 'tp'), as said below
- block_mask: int32 [64, 4], P('ctx'), may hold values from 0 to 1, as said below
- counter_base: int32 [2], replicated, may hold values from 0 to 1048575
- q_weight: bfloat16 [4096, 8192], P(None, 'tp'), may hold values from -0.125 to 0.125
- k_weight: bfloat16 [4096, 2048], P(None, 'tp'), may hold values from -0.09375 to 0.09375
- v_weight: bfloat16 [4096, 2048], P(None, 'tp'), may hold values from -0.09375 to 0.09375
Outputs:
- input_grad: bfloat16 [16384, 4096], P('ctx', 'tp')
The draws below stay inside these ranges and needn't reach their ends.
Inputs may be any that keep to these rules, and one draw needn't show every extreme that they name: block_mask[i, r] is 1 where query block i attends to key block i - r; column 0 and the row of the last block are all 1. log_norm lies between log(512) - 0.5 and log(512) + 2.5.
All inputs are finite; a program needn't handle non-finite values.
Results may differ from the reference program's by a relative error of at most 0.015.
Values may be sent and summed in bfloat16 or wider, within the bound.
A program may use at most 32 MiB of HBM per device.

```python
import math
import jax
import jax.numpy as jnp
from jax import lax

TOK = 256
D = 4096
HD = 128
HQ_DEV = 4
STEPS = 4
NBLK = 64
SEQ = 16384
HEADS = 64
WIN = 896
N_TP = 16


def draw_log_norm(key, part):
    centre = math.log(2.0 * TOK)
    spread = jax.random.uniform(key, (SEQ, HEADS), jnp.float32, 0.0, 1.5)
    return (centre + spread).astype(jnp.float32)


def draw_block_mask(key, part):
    random_bits = jax.random.randint(key, (NBLK, STEPS), 0, 2, dtype=jnp.int32)
    first_col = jnp.arange(STEPS, dtype=jnp.int32)[None, :] == 0
    last_row = jnp.arange(NBLK, dtype=jnp.int32)[:, None] == NBLK - 1
    return jnp.where(first_col | last_row, jnp.int32(1), random_bits).astype(jnp.int32)


def raised(result, key, source, target, parts, factor):
    owner, partner = [(jnp.arange(result.shape[position]) // (result.shape[position] // parts)).reshape([-1 if axis == position else 1 for axis in range(result.ndim)]) for position in (source, target)]
    chosen = jax.random.permutation(key, parts)[partner]
    strong = (owner == chosen) | (owner == (partner + parts // 2) % parts)
    return jnp.where(strong, factor * result, result)


def shard_levels(rng, dims, cuts, smallest, top_value):
    factor_of = 1.0
    for axis_at, blocks in cuts:
        draws = jax.random.uniform(jax.random.fold_in(jax.random.fold_in(rng, 6), axis_at), (blocks,), jnp.float32, smallest / len(cuts), top_value / len(cuts))
        factor_of = factor_of * jnp.repeat(jnp.exp(draws), dims[axis_at] // blocks).reshape((-1,) + (1,) * (len(dims) - 1 - axis_at))
    return factor_of


def bell_draw(own_key, extent, deviation, reach, cuts=(), held_as=jnp.bfloat16):
    values = jax.random.normal(own_key, extent, jnp.float32) * deviation
    if len(cuts) > 0:
        values = shard_levels(own_key, extent, cuts, -0.22, 0.18) * values
    return jnp.clip(values, min=-reach, max=reach).astype(held_as)


def heavy_noise(stream_key, extent, scale, most, cuts, heavy, kind=jnp.bfloat16):
    result = scale * jax.random.normal(stream_key, extent, jnp.float32)
    if cuts:
        result = result * shard_levels(stream_key, extent, cuts, -0.22, 0.18)
    return jnp.clip(raised(result, jax.random.fold_in(stream_key, 3), *heavy), -most, most).astype(kind)


def setup_inputs(seed: int = 0) -> dict:
    splits = jax.random.split(jax.random.key(seed), 12)
    queries = bell_draw(splits[0], (SEQ, HEADS * HD), 1.0, 6.0, ((0, 64), (1, 16)))
    keys = bell_draw(splits[1], (SEQ, N_TP * HD), 1.0, 6.0, ((0, 64), (1, 16)))
    values = bell_draw(splits[2], (SEQ, N_TP * HD), 1.0, 6.0, ((0, 64), (1, 16)))
    outputs = bell_draw(splits[3], (SEQ, HEADS * HD), 1.0, 6.0, ((0, 64), (1, 16)))
    out_grad = bell_draw(splits[4], (SEQ, HEADS * HD), 1.0, 6.0, ((0, 64), (1, 16)))
    log_norm = draw_log_norm(jax.random.fold_in(splits[11], 71), 0)
    block_mask = draw_block_mask(jax.random.fold_in(splits[11], 71), 0)
    counter_base = jax.random.randint(splits[7], (2,), 0, 1048576).astype(jnp.int32)
    q_weight = heavy_noise(splits[8], (D, HEADS * HD), D ** -0.5, 0.125, ((1, 16),), (1, 0, 16, 2.0))
    k_weight = bell_draw(splits[9], (D, N_TP * HD), D ** -0.5, 0.09375, ((1, 16),))
    v_weight = bell_draw(splits[10], (D, N_TP * HD), D ** -0.5, 0.09375, ((1, 16),))
    return {"queries": queries, "keys": keys, "values": values, "outputs": outputs, "out_grad": out_grad, "log_norm": log_norm, "block_mask": block_mask, "counter_base": counter_base, "q_weight": q_weight, "k_weight": k_weight, "v_weight": v_weight}


keep_level = 103
keep_scale = 1024.0 / 921.0


def keep_mask(head_ids, query_pos, key_pos, seed_value):
    mixed = head_ids[:, None, None] * 83492791 + query_pos[None, :, None] * 73856093 + key_pos[None, None, :] * 19349663 + seed_value
    mixed = mixed ^ lax.shift_right_logical(mixed, jnp.int32(15))
    mixed = mixed * 739982445
    mixed = mixed ^ lax.shift_right_logical(mixed, jnp.int32(12))
    mixed = mixed * 695872825
    mixed = mixed ^ lax.shift_right_logical(mixed, jnp.int32(15))
    return (mixed & 1023) >= keep_level


def pair_grads(query_blk, grad_out, norm_blk, row_delta, key_blk, value_blk, query_start, key_start, active, head_ids, counter_base, window):
    rows_count = query_blk.shape[0]
    scaling = query_blk.shape[2] ** -0.5
    scores = jnp.einsum("qhd,kd->hqk", query_blk.astype(jnp.float32), key_blk.astype(jnp.float32)) * scaling
    query_pos = query_start + jnp.arange(rows_count, dtype=jnp.int32)
    key_pos = key_start + jnp.arange(rows_count, dtype=jnp.int32)
    spacing = query_pos[:, None] - key_pos[None, :]
    allowed = (spacing >= 0) & (spacing < window) & active
    probs = jnp.where(allowed[None], jnp.exp(scores - jnp.transpose(norm_blk)[:, :, None]), jnp.float32(0.0))
    kept = keep_mask(head_ids, query_pos + counter_base[1], key_pos + counter_base[1], counter_base[0])
    dropped = jnp.where(kept, probs * keep_scale, jnp.float32(0.0)).astype(jnp.bfloat16)
    grad_value = jnp.einsum("hqk,qhd->kd", dropped.astype(jnp.float32), grad_out.astype(jnp.float32))
    grad_probs = jnp.einsum("qhd,kd->hqk", grad_out.astype(jnp.float32), value_blk.astype(jnp.float32))
    grad_scores = (probs * (jnp.where(kept, grad_probs * keep_scale, jnp.float32(0.0)) - jnp.transpose(row_delta)[:, :, None])).astype(jnp.bfloat16)
    grad_query = jnp.einsum("hqk,kd->qhd", grad_scores.astype(jnp.float32), key_blk.astype(jnp.float32)) * scaling
    grad_key = jnp.einsum("hqk,qhd->kd", grad_scores.astype(jnp.float32), query_blk.astype(jnp.float32)) * scaling
    return grad_query, grad_key, grad_value


def by_group(array, inner_cols):
    return jnp.transpose(array.reshape(array.shape[0], N_TP, inner_cols), (1, 0, 2))


def reference(queries, keys, values, outputs, out_grad, log_norm, block_mask, counter_base, q_weight, k_weight, v_weight):
    seq_len = NBLK * TOK
    head_width = HQ_DEV * HD
    grouped = (by_group(queries, head_width), by_group(keys, HD), by_group(values, HD), by_group(outputs, head_width), by_group(out_grad, head_width), by_group(log_norm, HQ_DEV), by_group(q_weight, head_width), by_group(k_weight, HD), by_group(v_weight, HD), jnp.arange(N_TP, dtype=jnp.int32))

    def group_step(summed, pieces):
        query_g, key_g, value_g, output_g, grad_g, norm_g, weight_q, weight_k, weight_v, group_id = pieces
        query_blocks = query_g.reshape(NBLK, TOK, HQ_DEV, HD)
        grad_blocks = grad_g.reshape(NBLK, TOK, HQ_DEV, HD)
        delta_all = jnp.sum(grad_g.astype(jnp.float32).reshape(seq_len, HQ_DEV, HD) * output_g.astype(jnp.float32).reshape(seq_len, HQ_DEV, HD), axis=2)
        delta_blocks = delta_all.reshape(NBLK, TOK, HQ_DEV)
        norm_blocks = norm_g.reshape(NBLK, TOK, HQ_DEV)
        key_blocks = key_g.reshape(NBLK, TOK, HD)
        value_blocks = value_g.reshape(NBLK, TOK, HD)
        head_ids = group_id * HQ_DEV + jnp.arange(HQ_DEV, dtype=jnp.int32)

        def per_block(block_id):
            grad_query = jnp.zeros((TOK, HQ_DEV, HD), jnp.float32)
            key_terms = []
            value_terms = []
            for offset in range(STEPS):
                source = jnp.maximum(block_id - offset, 0).astype(jnp.int32)
                active = (block_id - offset >= 0) & (block_mask[block_id, offset] == 1)
                add_query, add_key, add_value = pair_grads(query_blocks[block_id], grad_blocks[block_id], norm_blocks[block_id], delta_blocks[block_id], key_blocks[source], value_blocks[source], block_id * TOK, source * TOK, active, head_ids, counter_base, WIN)
                grad_query = grad_query + add_query
                key_terms.append(add_key)
                value_terms.append(add_value)
            return grad_query, jnp.stack(key_terms), jnp.stack(value_terms)

        grad_query, key_contrib, value_contrib = lax.map(per_block, jnp.arange(NBLK, dtype=jnp.int32))
        grad_key = jnp.zeros((NBLK, TOK, HD), jnp.float32)
        grad_value = jnp.zeros((NBLK, TOK, HD), jnp.float32)
        for offset in range(STEPS):
            padding = jnp.zeros((offset, TOK, HD), jnp.float32)
            grad_key = grad_key + jnp.concatenate([key_contrib[offset:, offset], padding], axis=0)
            grad_value = grad_value + jnp.concatenate([value_contrib[offset:, offset], padding], axis=0)
        query_round = grad_query.reshape(seq_len, head_width).astype(jnp.bfloat16)
        key_round = grad_key.reshape(seq_len, HD).astype(jnp.bfloat16)
        value_round = grad_value.reshape(seq_len, HD).astype(jnp.bfloat16)
        partial_term = jnp.dot(query_round, weight_q.T, preferred_element_type=jnp.float32)
        partial_term = partial_term + jnp.dot(key_round, weight_k.T, preferred_element_type=jnp.float32)
        partial_term = partial_term + jnp.dot(value_round, weight_v.T, preferred_element_type=jnp.float32)
        rounded = lax.optimization_barrier(partial_term.astype(jnp.bfloat16))
        return summed + rounded.astype(jnp.float32), None

    summed, unused = lax.scan(group_step, jnp.zeros((seq_len, D), jnp.float32), grouped)
    return summed.astype(jnp.bfloat16)
```

```python
import functools

import jax
import jax.numpy as jnp
from jax import lax
from jax.experimental import pallas as pl
from jax.experimental.pallas import tpu as pltpu
from jax.sharding import PartitionSpec as P

MESH = pl.DeviceIdType.MESH
keep_level = 103
keep_scale = 1024.0 / 921.0
ROWS = 16
NT = (((1,), (1,)), ((), ()))
NN = (((1,), (0,)), ((), ()))
TN = (((0,), (0,)), ((), ()))
HOPS = ((2, 1), (2, 0), (1, 1), (3, 1), (0, 1), (1, 0), (3, 0), (0, 0))
OFFSETS = (2, 1, 3, 0)


def dot(a, b, dims):
    return lax.dot_general(a, b, dims, preferred_element_type=jnp.float32)


def kernel(
    q_hbm,
    k_hbm,
    v_hbm,
    o_hbm,
    g_hbm,
    norm_hbm,
    mask_smem,
    base_smem,
    wq_hbm,
    wk_hbm,
    wv_hbm,
    out_ref,
    q_st,
    g_st,
    o_st,
    norm_in,
    own_kv,
    got_kv,
    kept,
    s_buf,
    dp_buf,
    pk_buf,
    ds_buf,
    rows_buf,
    dq_acc,
    own_acc,
    back_out,
    back_in,
    grads,
    kv_grads,
    wq,
    wkv,
    terms,
    pair_out,
    pair_in,
    far_out,
    far_in,
    load_sem,
    kv_send,
    kv_recv,
    back_send,
    back_recv,
    pair_send,
    pair_recv,
    far_send,
    far_recv,
):
    tok = k_hbm.shape[0]
    hd = k_hbm.shape[1]
    heads = q_hbm.shape[1] // hd
    wide = heads * tok
    blocks = lax.axis_size("ctx")
    block_id = lax.axis_index("ctx")
    group_id = lax.axis_index("tp")
    y_pos = group_id // 4
    x_pos = (group_id // 2) % 2
    core = group_id % 2
    scaling = hd ** (-0.5)

    def ctx_at(steps):
        return lax.rem(block_id + steps + blocks, blocks)

    def chip_at(hop):
        return lax.rem(y_pos + hop[0], 4) * 2 + lax.rem(x_pos + hop[1], 2)

    partner = group_id + 1 - 2 * core

    loads = []

    def load(src, dst):
        copy = pltpu.make_async_copy(src, dst, load_sem.at[len(loads)])
        copy.start()
        loads.append(copy)
        return copy

    kv_loads = [load(k_hbm, own_kv.at[0]), load(v_hbm, own_kv.at[1])]
    head_loads = []
    for src, dst in ((g_hbm, g_st), (o_hbm, o_st), (q_hbm, q_st)):
        for h in range(heads):
            head_loads.append(
                load(src.at[:, pl.ds(h * hd, hd)], dst.at[pl.ds(h * tok, tok), :])
            )
    norm_load = load(norm_hbm, norm_in)
    weight_loads = [
        load(wq_hbm, wq),
        load(wk_hbm, wkv.at[:, pl.ds(0, hd)]),
        load(wv_hbm, wkv.at[:, pl.ds(hd, hd)]),
    ]

    barrier = pltpu.get_barrier_semaphore()
    peers = [(ctx_at(r), group_id) for r in (1, -1, 2, -2, 3, -3)]
    peers.append((block_id, partner))
    peers += [(block_id, chip_at(hop) * 2 + core) for hop in HOPS[:-1]]
    for peer in peers:
        pl.semaphore_signal(barrier, inc=1, device_id=peer, device_id_type=MESH)
    pl.semaphore_wait(barrier, len(peers))

    for copy in kv_loads:
        copy.wait()
    kv_copies = {}
    for r in (1, 2, 3):
        for part in range(2):
            copy = pltpu.make_async_remote_copy(
                src_ref=own_kv.at[part],
                dst_ref=got_kv.at[r - 1, part],
                send_sem=kv_send.at[r - 1, part],
                recv_sem=kv_recv.at[r - 1, part],
                device_id=(ctx_at(r), group_id),
                device_id_type=MESH,
            )
            kv_copies[r, part] = copy
    for r in (2, 1, 3):
        for part in range(2):
            kv_copies[r, part].start()

    lane = lax.broadcasted_iota(jnp.int32, (ROWS, wide), 1)
    sub = lax.broadcasted_iota(jnp.int32, (ROWS, wide), 0)
    head = lane // tok
    query = lane - head * tok
    spread = query - sub
    seed = base_smem[0]
    shift = base_smem[1]
    mixed_base = (
        (head + group_id * heads) * 83492791
        + query * 73856093
        + sub * 19349663
        + ((block_id * tok + shift) * 73856093 + seed)
    )

    def mask_rows(r):
        def step(i, carry):
            key_start = (block_id - r) * tok + i * ROWS + shift
            mixed = mixed_base + key_start * 19349663
            mixed = mixed ^ lax.shift_right_logical(mixed, jnp.int32(15))
            mixed = mixed * 739982445
            mixed = mixed ^ lax.shift_right_logical(mixed, jnp.int32(12))
            mixed = mixed * 695872825
            mixed = mixed ^ lax.shift_right_logical(mixed, jnp.int32(15))
            kept[r, pl.ds(pl.multiple_of(i * ROWS, ROWS), ROWS), :] = jnp.where(
                mixed & 1023 >= keep_level, jnp.float32(1.0), jnp.float32(0.0)
            )
            return carry

        lax.fori_loop(0, tok // ROWS, step, 0)

    for r in OFFSETS:
        mask_rows(r)

    for copy in head_loads:
        copy.wait()
    norm_load.wait()
    for h in range(heads):
        rows = pl.ds(h * tok, tok)
        prod = g_st[rows, :].astype(jnp.float32) * o_st[rows, :].astype(jnp.float32)
        delta = jnp.sum(jnp.transpose(prod), axis=0, keepdims=True)
        rows_buf[0:1, rows] = delta * jnp.float32(1.0 / keep_scale)
        column = jnp.broadcast_to(norm_in[:, h : h + 1], (tok, hd))
        norm_row = jnp.transpose(column)[0:1, :]
        for r in range(4):
            active = (block_id - r >= 0) & (mask_smem[0, r] == 1)
            push = jnp.where(active, jnp.float32(0.0), jnp.float32(1e30))
            rows_buf[r + 1 : r + 2, rows] = norm_row + push

    back_copies = {}
    for place, r in enumerate(OFFSETS):
        if r > 0:
            for part in range(2):
                kv_copies[r, part].wait_recv()
            key_blk = got_kv.at[r - 1, 0]
            value_blk = got_kv.at[r - 1, 1]
        else:
            key_blk = own_kv.at[0]
            value_blk = own_kv.at[1]
        s_buf[...] = dot(key_blk[...], q_st[...], NT)
        dp_buf[...] = dot(value_blk[...], g_st[...], NT)

        def pair_rows(i, carry, r=r):
            at = pl.ds(pl.multiple_of(i * ROWS, ROWS), ROWS)
            probs = jnp.exp(s_buf[at, :] * jnp.float32(scaling) - rows_buf[r + 1 : r + 2, :])
            if r == 0:
                probs = jnp.where(spread >= i * ROWS, probs, jnp.float32(0.0))
            if r == 3:
                probs = jnp.where(spread < i * ROWS + tok // 2, probs, jnp.float32(0.0))
            dropped = probs * kept[r, at, :]
            pk_buf[at, :] = dropped.astype(jnp.bfloat16)
            ds_buf[at, :] = (dropped * dp_buf[at, :] - probs * rows_buf[0:1, :]).astype(
                jnp.bfloat16
            )
            return carry

        lax.fori_loop(0, tok // ROWS, pair_rows, 0)
        add_value = dot(pk_buf[...], g_st[...], NN) * jnp.float32(keep_scale)
        add_key = dot(ds_buf[...], q_st[...], NN) * jnp.float32(keep_scale * scaling)
        if r > 0:
            back_out[r - 1, 0] = add_key.astype(jnp.bfloat16)
            back_out[r - 1, 1] = add_value.astype(jnp.bfloat16)
            for part in range(2):
                copy = pltpu.make_async_remote_copy(
                    src_ref=back_out.at[r - 1, part],
                    dst_ref=back_in.at[r - 1, part],
                    send_sem=back_send.at[r - 1, part],
                    recv_sem=back_recv.at[r - 1, part],
                    device_id=(ctx_at(-r), group_id),
                    device_id_type=MESH,
                )
                copy.start()
                back_copies[r, part] = copy
        else:
            own_acc[0] = add_key
            own_acc[1] = add_value
        add_query = dot(key_blk[...], ds_buf[...], TN)
        if place == 0:
            dq_acc[...] = add_query
        else:
            dq_acc[...] += add_query

    for h in range(heads):
        part_t = jnp.transpose(dq_acc[:, pl.ds(h * tok, tok)])
        grads[:, pl.ds(h * hd, hd)] = (part_t * jnp.float32(keep_scale * scaling)).astype(
            jnp.bfloat16
        )

    for copy in weight_loads:
        copy.wait()

    def query_terms(i, carry):
        at = pl.ds(pl.multiple_of(i * tok, tok), tok)
        terms[i] = dot(grads[...], wq[at, :], NT)
        return carry

    lax.fori_loop(0, 16, query_terms, 0)

    for r in (2, 1, 3):
        for part in range(2):
            back_copies[r, part].wait_recv()
    for part in range(2):
        total = own_acc[part]
        for r in (1, 2, 3):
            total = total + back_in[r - 1, part].astype(jnp.float32)
        kv_grads[:, pl.ds(part * hd, hd)] = total.astype(jnp.bfloat16)

    def term(index):
        at = pl.ds(pl.multiple_of(index * tok, tok), tok)
        return terms[index] + dot(kv_grads[...], wkv[at, :], NT)

    pair_copies = []

    def send_pair(j):
        pair_out[j] = term(chip_at(HOPS[j]) * 2 + 1 - core).astype(jnp.bfloat16)
        copy = pltpu.make_async_remote_copy(
            src_ref=pair_out.at[j],
            dst_ref=pair_in.at[j],
            send_sem=pair_send.at[j],
            recv_sem=pair_recv.at[j],
            device_id=(block_id, partner),
            device_id_type=MESH,
        )
        copy.start()
        pair_copies.append(copy)

    far_copies = []
    send_pair(0)
    send_pair(1)
    for j in range(8):
        if j + 2 < 8:
            send_pair(j + 2)
        index = chip_at(HOPS[j]) * 2 + core
        own = term(index)
        pair_copies[j].wait_recv()
        own = own + pair_in[j].astype(jnp.float32)
        if j < 7:
            far_out[j] = own.astype(jnp.bfloat16)
            copy = pltpu.make_async_remote_copy(
                src_ref=far_out.at[j],
                dst_ref=far_in.at[j],
                send_sem=far_send.at[j],
                recv_sem=far_recv.at[j],
                device_id=(block_id, index),
                device_id_type=MESH,
            )
            copy.start()
            far_copies.append(copy)
        else:
            terms[0] = own

    for copy in far_copies:
        copy.wait_recv()

    def last_rows(i, carry):
        at = pl.ds(pl.multiple_of(i * ROWS, ROWS), ROWS)
        total = terms[0, at, :]
        for j in range(7):
            total = total + far_in[j, at, :].astype(jnp.float32)
        out_ref[at, :] = total.astype(jnp.bfloat16)
        return carry

    lax.fori_loop(0, tok // ROWS, last_rows, 0)

    for copy in list(kv_copies.values()) + list(back_copies.values()) + pair_copies + far_copies:
        copy.wait_send()


def on_device(*args):
    queries, keys, values, outputs, out_grad, log_norm = args[:6]
    block_mask, counter_base, q_weight, k_weight, v_weight = args[6:]
    tok, hd = keys.shape
    heads = log_norm.shape[1]
    wide = heads * tok
    width = q_weight.shape[0]
    any_spec = pl.BlockSpec(memory_space=pl.ANY)
    smem_spec = pl.BlockSpec(memory_space=pltpu.SMEM)
    bf16, f32 = jnp.bfloat16, jnp.float32
    dma = pltpu.SemaphoreType.DMA
    return pl.pallas_call(
        kernel,
        out_shape=jax.ShapeDtypeStruct((tok, width // 16), bf16),
        in_specs=[any_spec] * 6 + [smem_spec] * 2 + [any_spec] * 3,
        out_specs=pl.BlockSpec(memory_space=pltpu.VMEM),
        scratch_shapes=[
            pltpu.VMEM((wide, hd), bf16),
            pltpu.VMEM((wide, hd), bf16),
            pltpu.VMEM((wide, hd), bf16),
            pltpu.VMEM((tok, heads), f32),
            pltpu.VMEM((2, tok, hd), bf16),
            pltpu.VMEM((3, 2, tok, hd), bf16),
            pltpu.VMEM((4, tok, wide), f32),
            pltpu.VMEM((tok, wide), f32),
            pltpu.VMEM((tok, wide), f32),
            pltpu.VMEM((tok, wide), bf16),
            pltpu.VMEM((tok, wide), bf16),
            pltpu.VMEM((8, wide), f32),
            pltpu.VMEM((hd, wide), f32),
            pltpu.VMEM((2, tok, hd), f32),
            pltpu.VMEM((3, 2, tok, hd), bf16),
            pltpu.VMEM((3, 2, tok, hd), bf16),
            pltpu.VMEM((tok, heads * hd), bf16),
            pltpu.VMEM((tok, 2 * hd), bf16),
            pltpu.VMEM((width, heads * hd), bf16),
            pltpu.VMEM((width, 2 * hd), bf16),
            pltpu.VMEM((16, tok, width // 16), f32),
            pltpu.VMEM((8, tok, width // 16), bf16),
            pltpu.VMEM((8, tok, width // 16), bf16),
            pltpu.VMEM((7, tok, width // 16), bf16),
            pltpu.VMEM((7, tok, width // 16), bf16),
            dma((2 + 3 * heads + 1 + 3,)),
            dma((3, 2)),
            dma((3, 2)),
            dma((3, 2)),
            dma((3, 2)),
            dma((8,)),
            dma((8,)),
            dma((7,)),
            dma((7,)),
        ],
        compiler_params=pltpu.CompilerParams(
            collective_id=0,
            has_side_effects=True,
            vmem_limit_bytes=58 * 1024 * 1024,
        ),
    )(*args)


def solution(mesh):
    return jax.shard_map(
        on_device,
        mesh=mesh,
        in_specs=(
            P("ctx", "tp"),
            P("ctx", "tp"),
            P("ctx", "tp"),
            P("ctx", "tp"),
            P("ctx", "tp"),
            P("ctx", "tp"),
            P("ctx", None),
            P(),
            P(None, "tp"),
            P(None, "tp"),
            P(None, "tp"),
        ),
        out_specs=P("ctx", "tp"),
        check_vma=False,
    )
```

```python
import functools

import jax
import jax.numpy as jnp
from jax import lax
from jax.experimental import pallas as pl
from jax.experimental.pallas import tpu as pltpu
from jax.sharding import PartitionSpec as P

MESH = pl.DeviceIdType.MESH
keep_level = 103
keep_scale = 1024.0 / 921.0
ROWS = 16
NT = (((1,), (1,)), ((), ()))
NN = (((1,), (0,)), ((), ()))
TN = (((0,), (0,)), ((), ()))
HOPS = ((2, 1), (1, 1), (3, 1), (0, 1), (2, 0), (1, 0), (3, 0), (0, 0))
OFFSETS = (2, 1, 3, 0)


def dot(a, b, dims):
    return lax.dot_general(a, b, dims, preferred_element_type=jnp.float32)


def kernel(
    q_hbm,
    k_hbm,
    v_hbm,
    o_hbm,
    g_hbm,
    norm_hbm,
    mask_smem,
    base_smem,
    wq_hbm,
    wk_hbm,
    wv_hbm,
    out_ref,
    q_st,
    g_st,
    o_st,
    norm_in,
    own_kv,
    got_kv,
    kept,
    s_buf,
    dp_buf,
    pk_buf,
    ds_buf,
    rows_buf,
    dq_acc,
    own_acc,
    back_out,
    back_in,
    grads,
    kv_grads,
    wq,
    wkv,
    terms,
    sums,
    pair_out,
    pair_in,
    far_out,
    far_in,
    load_sem,
    kv_send,
    kv_recv,
    back_send,
    back_recv,
    pair_send,
    pair_recv,
    far_send,
    far_recv,
):
    tok = k_hbm.shape[0]
    hd = k_hbm.shape[1]
    heads = q_hbm.shape[1] // hd
    wide = heads * tok
    blocks = lax.axis_size("ctx")
    block_id = lax.axis_index("ctx")
    group_id = lax.axis_index("tp")
    y_pos = group_id // 4
    x_pos = (group_id // 2) % 2
    core = group_id % 2
    scaling = hd ** (-0.5)

    def ctx_at(steps):
        return lax.rem(block_id + steps + blocks, blocks)

    def chip_at(hop):
        return lax.rem(y_pos + hop[0], 4) * 2 + lax.rem(x_pos + hop[1], 2)

    partner = group_id + 1 - 2 * core
    parity = block_id % 2
    x_peer = block_id + 1 - 2 * parity

    loads = []

    def load(src, dst):
        copy = pltpu.make_async_copy(src, dst, load_sem.at[len(loads)])
        copy.start()
        loads.append(copy)
        return copy

    kv_loads = [load(k_hbm, own_kv.at[0]), load(v_hbm, own_kv.at[1])]
    head_loads = []
    for src, dst in ((g_hbm, g_st), (o_hbm, o_st), (q_hbm, q_st)):
        for h in range(heads):
            head_loads.append(
                load(src.at[:, pl.ds(h * hd, hd)], dst.at[pl.ds(h * tok, tok), :])
            )
    norm_load = load(norm_hbm, norm_in)
    weight_loads = [
        load(wq_hbm, wq),
        load(wk_hbm, wkv.at[:, pl.ds(0, hd)]),
        load(wv_hbm, wkv.at[:, pl.ds(hd, hd)]),
    ]

    barrier = pltpu.get_barrier_semaphore()
    peers = [(ctx_at(r), group_id) for r in (1, -1, 2, -2, 3, -3)]
    peers.append((block_id, partner))
    peers += [(block_id, chip_at(hop) * 2 + core) for hop in HOPS[3:7]]
    for peer in peers:
        pl.semaphore_signal(barrier, inc=1, device_id=peer, device_id_type=MESH)
    pl.semaphore_wait(barrier, len(peers))

    for copy in kv_loads:
        copy.wait()
    def kv_copy(r, part, src):
        return pltpu.make_async_remote_copy(
            src_ref=src.at[part],
            dst_ref=got_kv.at[r - 1, part],
            send_sem=kv_send.at[r - 1, part],
            recv_sem=kv_recv.at[r - 1, part],
            device_id=(x_peer if r == 1 else ctx_at(2), group_id),
            device_id_type=MESH,
        )

    def kv_wait(r, part):
        kv_copy(r, part, own_kv).wait_recv()

    for part in range(2):
        kv_copy(2, part, own_kv).start()

        @pl.when(parity == 0)
        def _():
            kv_copy(1, part, own_kv).start()

    lane = lax.broadcasted_iota(jnp.int32, (ROWS, wide), 1)
    sub = lax.broadcasted_iota(jnp.int32, (ROWS, wide), 0)
    head = lane // tok
    query = lane - head * tok
    spread = query - sub
    seed = base_smem[0]
    shift = base_smem[1]
    mixed_base = (
        (head + group_id * heads) * 83492791
        + query * 73856093
        + sub * 19349663
        + ((block_id * tok + shift) * 73856093 + seed)
    )

    def mask_rows(r):
        def step(i, carry):
            key_start = (block_id - r) * tok + i * ROWS + shift
            mixed = mixed_base + key_start * 19349663
            mixed = mixed ^ lax.shift_right_logical(mixed, jnp.int32(15))
            mixed = mixed * 739982445
            mixed = mixed ^ lax.shift_right_logical(mixed, jnp.int32(12))
            mixed = mixed * 695872825
            mixed = mixed ^ lax.shift_right_logical(mixed, jnp.int32(15))
            kept[r, pl.ds(pl.multiple_of(i * ROWS, ROWS), ROWS), :] = jnp.where(
                mixed & 1023 >= keep_level, jnp.float32(1.0), jnp.float32(0.0)
            )
            return carry

        lax.fori_loop(0, tok // ROWS, step, 0)

    for r in OFFSETS:
        mask_rows(r)

    for copy in head_loads:
        copy.wait()
    norm_load.wait()
    for h in range(heads):
        rows = pl.ds(h * tok, tok)
        prod = g_st[rows, :].astype(jnp.float32) * o_st[rows, :].astype(jnp.float32)
        delta = jnp.sum(jnp.transpose(prod), axis=0, keepdims=True)
        rows_buf[0:1, rows] = delta * jnp.float32(1.0 / keep_scale)
        for r in range(4):
            active = (block_id - r >= 0) & (mask_smem[0, r] == 1)
            push = jnp.where(active, jnp.float32(0.0), jnp.float32(1e30))
            rows_buf[r + 1 : r + 2, rows] = norm_in[h : h + 1, :] + push

    def pass_on():
        for part in range(2):
            kv_wait(1, part)
            kv_copy(3, part, got_kv.at[0]).start()

    for part in range(2):
        kv_wait(2, part)

        @pl.when(parity == 1)
        def _():
            kv_copy(1, part, got_kv.at[1]).start()

    @pl.when(parity == 1)
    def _():
        pass_on()

    back_copies = {}
    for place, r in enumerate(OFFSETS):
        if r == 1:

            @pl.when(parity == 0)
            def _():
                pass_on()

        if r == 3:
            for part in range(2):
                kv_wait(3, part)
        if r > 0:
            key_blk = got_kv.at[r - 1, 0]
            value_blk = got_kv.at[r - 1, 1]
        else:
            key_blk = own_kv.at[0]
            value_blk = own_kv.at[1]
        s_buf[...] = dot(key_blk[...], q_st[...], NT)
        dp_buf[...] = dot(value_blk[...], g_st[...], NT)

        def pair_rows(i, carry, r=r):
            at = pl.ds(pl.multiple_of(i * ROWS, ROWS), ROWS)
            probs = jnp.exp(s_buf[at, :] * jnp.float32(scaling) - rows_buf[r + 1 : r + 2, :])
            if r == 0:
                probs = jnp.where(spread >= i * ROWS, probs, jnp.float32(0.0))
            if r == 3:
                probs = jnp.where(spread < i * ROWS + tok // 2, probs, jnp.float32(0.0))
            dropped = probs * kept[r, at, :]
            pk_buf[at, :] = dropped.astype(jnp.bfloat16)
            ds_buf[at, :] = (dropped * dp_buf[at, :] - probs * rows_buf[0:1, :]).astype(
                jnp.bfloat16
            )
            return carry

        lax.fori_loop(0, tok // ROWS, pair_rows, 0)
        add_value = dot(pk_buf[...], g_st[...], NN) * jnp.float32(keep_scale)
        add_key = dot(ds_buf[...], q_st[...], NN) * jnp.float32(keep_scale * scaling)
        if r > 0:
            back_out[r - 1, 0] = add_key.astype(jnp.bfloat16)
            back_out[r - 1, 1] = add_value.astype(jnp.bfloat16)
            for part in range(2):
                copy = pltpu.make_async_remote_copy(
                    src_ref=back_out.at[r - 1, part],
                    dst_ref=back_in.at[r - 1, part],
                    send_sem=back_send.at[r - 1, part],
                    recv_sem=back_recv.at[r - 1, part],
                    device_id=(ctx_at(-r), group_id),
                    device_id_type=MESH,
                )
                copy.start()
                back_copies[r, part] = copy
        else:
            own_acc[0] = add_key
            own_acc[1] = add_value
        add_query = dot(key_blk[...], ds_buf[...], TN)
        if place == 0:
            dq_acc[...] = add_query
        else:
            dq_acc[...] += add_query

    for h in range(heads):
        part_t = jnp.transpose(dq_acc[:, pl.ds(h * tok, tok)])
        grads[:, pl.ds(h * hd, hd)] = (part_t * jnp.float32(keep_scale * scaling)).astype(
            jnp.bfloat16
        )

    for copy in weight_loads:
        copy.wait()

    def query_terms(i, carry):
        at = pl.ds(pl.multiple_of(i * tok, tok), tok)
        terms[i] = dot(grads[...], wq[at, :], NT)
        return carry

    lax.fori_loop(0, 16, query_terms, 0)

    for r in (2, 1, 3):
        for part in range(2):
            back_copies[r, part].wait_recv()
    for part in range(2):
        total = own_acc[part]
        for r in (1, 2, 3):
            total = total + back_in[r - 1, part].astype(jnp.float32)
        kv_grads[:, pl.ds(part * hd, hd)] = total.astype(jnp.bfloat16)

    def term(index):
        at = pl.ds(pl.multiple_of(index * tok, tok), tok)
        return terms[index] + dot(kv_grads[...], wkv[at, :], NT)

    pair_copies = []

    def send_pair(j):
        pair_out[j] = term(chip_at(HOPS[j]) * 2 + 1 - core).astype(jnp.bfloat16)
        copy = pltpu.make_async_remote_copy(
            src_ref=pair_out.at[j],
            dst_ref=pair_in.at[j],
            send_sem=pair_send.at[j],
            recv_sem=pair_recv.at[j],
            device_id=(block_id, partner),
            device_id_type=MESH,
        )
        copy.start()
        pair_copies.append(copy)

    def far_copy(j):
        if j < 3:
            hop_y, hop_x = core * HOPS[j][0], 1 - core
        else:
            hop_y, hop_x = HOPS[j][0], HOPS[j][1]
        return pltpu.make_async_remote_copy(
            src_ref=far_out.at[j],
            dst_ref=far_in.at[j],
            send_sem=far_send.at[j],
            recv_sem=far_recv.at[j],
            device_id=(block_id, chip_at((hop_y, hop_x)) * 2 + core),
            device_id_type=MESH,
        )

    def send_far(j, value):
        far_out[j] = value.astype(jnp.bfloat16)
        far_copy(j).start()

    send_pair(0)
    send_pair(1)
    for j in range(8):
        if j + 2 < 8:
            send_pair(j + 2)
        own = term(chip_at(HOPS[j]) * 2 + core)
        pair_copies[j].wait_recv()
        own = own + pair_in[j].astype(jnp.float32)
        if j < 3:
            send_far(j, own)
        else:
            sums[j - 3] = own
        if 3 <= j < 7:

            @pl.when(core == (0 if j == 3 else 1))
            def _():
                send_far(j, sums[j - 3])

    @pl.when(core == 0)
    def _():
        for j in range(3):
            far_copy(j).wait_recv()
            send_far(j + 4, sums[j + 1] + far_in[j].astype(jnp.float32))

    @pl.when(core == 1)
    def _():
        total = sums[0]
        for j in range(3):
            far_copy(j).wait_recv()
            total = total + far_in[j].astype(jnp.float32)
        send_far(3, total)

    for j in (4, 5, 6, 3):
        far_copy(j).wait_recv()

    def last_rows(i, carry):
        at = pl.ds(pl.multiple_of(i * ROWS, ROWS), ROWS)
        total = sums[4, at, :]
        for j in range(3, 7):
            total = total + far_in[j, at, :].astype(jnp.float32)
        out_ref[at, :] = total
        return carry

    lax.fori_loop(0, tok // ROWS, last_rows, 0)

    sent = [kv_copy(r, part, own_kv) for r in (1, 2, 3) for part in range(2)]
    sent += list(back_copies.values()) + pair_copies + [far_copy(j) for j in range(7)]
    for copy in sent:
        copy.wait_send()


def on_device(*args):
    queries, keys, values, outputs, out_grad, log_norm = args[:6]
    q_weight = args[8]
    tok, hd = keys.shape
    heads = log_norm.shape[1]
    wide = heads * tok
    width = q_weight.shape[0]
    any_spec = pl.BlockSpec(memory_space=pl.ANY)
    smem_spec = pl.BlockSpec(memory_space=pltpu.SMEM)
    bf16, f32 = jnp.bfloat16, jnp.float32
    dma = pltpu.SemaphoreType.DMA
    total = pl.pallas_call(
        kernel,
        out_shape=jax.ShapeDtypeStruct((tok, width // 16), f32),
        in_specs=[any_spec] * 6 + [smem_spec] * 2 + [any_spec] * 3,
        out_specs=pl.BlockSpec(memory_space=pltpu.VMEM),
        scratch_shapes=[
            pltpu.VMEM((wide, hd), bf16),
            pltpu.VMEM((wide, hd), bf16),
            pltpu.VMEM((wide, hd), bf16),
            pltpu.VMEM((heads, tok), f32),
            pltpu.VMEM((2, tok, hd), bf16),
            pltpu.VMEM((3, 2, tok, hd), bf16),
            pltpu.VMEM((4, tok, wide), f32),
            pltpu.VMEM((tok, wide), f32),
            pltpu.VMEM((tok, wide), f32),
            pltpu.VMEM((tok, wide), bf16),
            pltpu.VMEM((tok, wide), bf16),
            pltpu.VMEM((8, wide), f32),
            pltpu.VMEM((hd, wide), f32),
            pltpu.VMEM((2, tok, hd), f32),
            pltpu.VMEM((3, 2, tok, hd), bf16),
            pltpu.VMEM((3, 2, tok, hd), bf16),
            pltpu.VMEM((tok, heads * hd), bf16),
            pltpu.VMEM((tok, 2 * hd), bf16),
            pltpu.VMEM((width, heads * hd), bf16),
            pltpu.VMEM((width, 2 * hd), bf16),
            pltpu.VMEM((16, tok, width // 16), f32),
            pltpu.VMEM((5, tok, width // 16), f32),
            pltpu.VMEM((8, tok, width // 16), bf16),
            pltpu.VMEM((8, tok, width // 16), bf16),
            pltpu.VMEM((7, tok, width // 16), bf16),
            pltpu.VMEM((7, tok, width // 16), bf16),
            dma((2 + 3 * heads + 1 + 3,)),
            dma((3, 2)),
            dma((3, 2)),
            dma((3, 2)),
            dma((3, 2)),
            dma((8,)),
            dma((8,)),
            dma((7,)),
            dma((7,)),
        ],
        compiler_params=pltpu.CompilerParams(
            collective_id=0,
            has_side_effects=True,
            vmem_limit_bytes=58 * 1024 * 1024,
        ),
    )(queries, keys, values, outputs, out_grad, log_norm.T, *args[6:])
    return total.astype(bf16)


def solution(mesh):
    return jax.shard_map(
        on_device,
        mesh=mesh,
        in_specs=(
            P("ctx", "tp"),
            P("ctx", "tp"),
            P("ctx", "tp"),
            P("ctx", "tp"),
            P("ctx", "tp"),
            P("ctx", "tp"),
            P("ctx", None),
            P(),
            P(None, "tp"),
            P(None, "tp"),
            P(None, "tp"),
        ),
        out_specs=P("ctx", "tp"),
        check_vma=False,
    )
```

```python
import functools

import jax
import jax.numpy as jnp
from jax import lax
from jax.experimental import pallas as pl
from jax.experimental.pallas import tpu as pltpu
from jax.sharding import PartitionSpec as P

MESH = pl.DeviceIdType.MESH
keep_level = 103
keep_scale = 1024.0 / 921.0
ROWS = 16
NT = (((1,), (1,)), ((), ()))
NN = (((1,), (0,)), ((), ()))
TN = (((0,), (0,)), ((), ()))
HOPS = ((2, 1), (1, 1), (3, 1), (0, 1), (2, 0), (1, 0), (3, 0), (0, 0))
OFFSETS = (2, 1, 3, 0)


def dot(a, b, dims):
    return lax.dot_general(a, b, dims, preferred_element_type=jnp.float32)


def kernel(
    q_hbm,
    k_hbm,
    v_hbm,
    o_hbm,
    g_hbm,
    norm_hbm,
    mask_smem,
    base_smem,
    wq_hbm,
    wk_hbm,
    wv_hbm,
    out_ref,
    q_st,
    g_st,
    o_st,
    norm_in,
    own_kv,
    got_kv,
    kept,
    s_buf,
    dp_buf,
    pk_buf,
    ds_buf,
    rows_buf,
    dq_acc,
    own_acc,
    back_out,
    back_in,
    grads,
    kv_grads,
    wq,
    wkv,
    terms,
    sums,
    pair_out,
    pair_in,
    far_out,
    far_in,
    load_sem,
    kv_send,
    kv_recv,
    back_send,
    back_recv,
    pair_send,
    pair_recv,
    far_send,
    far_recv,
):
    tok = k_hbm.shape[0]
    hd = k_hbm.shape[1]
    heads = q_hbm.shape[1] // hd
    wide = heads * tok
    half_rows = tok // 2
    halves = [pl.ds(half * half_rows, half_rows) for half in range(2)]
    blocks = lax.axis_size("ctx")
    block_id = lax.axis_index("ctx")
    group_id = lax.axis_index("tp")
    y_pos = group_id // 4
    x_pos = (group_id // 2) % 2
    core = group_id % 2
    scaling = hd ** (-0.5)

    def ctx_at(steps):
        return lax.rem(block_id + steps + blocks, blocks)

    def chip_at(hop):
        return lax.rem(y_pos + hop[0], 4) * 2 + lax.rem(x_pos + hop[1], 2)

    partner = group_id + 1 - 2 * core
    parity = block_id % 2
    x_peer = block_id + 1 - 2 * parity

    loads = []

    def load(src, dst):
        copy = pltpu.make_async_copy(src, dst, load_sem.at[len(loads)])
        copy.start()
        loads.append(copy)
        return copy

    kv_loads = [load(k_hbm, own_kv.at[0]), load(v_hbm, own_kv.at[1])]
    head_loads = []
    for src, dst in ((g_hbm, g_st), (o_hbm, o_st), (q_hbm, q_st)):
        for h in range(heads):
            head_loads.append(
                load(src.at[:, pl.ds(h * hd, hd)], dst.at[pl.ds(h * tok, tok), :])
            )
    norm_load = load(norm_hbm, norm_in)
    weight_loads = [
        load(wq_hbm, wq),
        load(wk_hbm, wkv.at[:, pl.ds(0, hd)]),
        load(wv_hbm, wkv.at[:, pl.ds(hd, hd)]),
    ]

    barrier = pltpu.get_barrier_semaphore()
    peers = [(ctx_at(r), group_id) for r in (1, -1, 2, -2, 3, -3)]
    peers.append((block_id, partner))
    peers += [(block_id, chip_at(hop) * 2 + core) for hop in HOPS[3:7]]
    for peer in peers:
        pl.semaphore_signal(barrier, inc=1, device_id=peer, device_id_type=MESH)
    pl.semaphore_wait(barrier, len(peers))

    for copy in kv_loads:
        copy.wait()
    def kv_copy(r, part, src):
        return pltpu.make_async_remote_copy(
            src_ref=src.at[part],
            dst_ref=got_kv.at[r - 1, part],
            send_sem=kv_send.at[r - 1, part],
            recv_sem=kv_recv.at[r - 1, part],
            device_id=(x_peer if r == 1 else ctx_at(2), group_id),
            device_id_type=MESH,
        )

    def kv_wait(r, part):
        kv_copy(r, part, own_kv).wait_recv()

    for part in range(2):
        kv_copy(2, part, own_kv).start()

        @pl.when(parity == 0)
        def _():
            kv_copy(1, part, own_kv).start()

    lane = lax.broadcasted_iota(jnp.int32, (ROWS, wide), 1)
    sub = lax.broadcasted_iota(jnp.int32, (ROWS, wide), 0)
    head = lane // tok
    query = lane - head * tok
    spread = query - sub
    seed = base_smem[0]
    shift = base_smem[1]
    mixed_base = (
        (head + group_id * heads) * 83492791
        + query * 73856093
        + sub * 19349663
        + ((block_id * tok + shift) * 73856093 + seed)
    )

    def mask_rows(r):
        def step(i, carry):
            key_start = (block_id - r) * tok + i * ROWS + shift
            mixed = mixed_base + key_start * 19349663
            mixed = mixed ^ lax.shift_right_logical(mixed, jnp.int32(15))
            mixed = mixed * 739982445
            mixed = mixed ^ lax.shift_right_logical(mixed, jnp.int32(12))
            mixed = mixed * 695872825
            mixed = mixed ^ lax.shift_right_logical(mixed, jnp.int32(15))
            kept[r, pl.ds(pl.multiple_of(i * ROWS, ROWS), ROWS), :] = jnp.where(
                mixed & 1023 >= keep_level, jnp.float32(1.0), jnp.float32(0.0)
            )
            return carry

        lax.fori_loop(0, tok // ROWS, step, 0)

    for r in OFFSETS:
        mask_rows(r)

    for copy in head_loads:
        copy.wait()
    norm_load.wait()
    for h in range(heads):
        rows = pl.ds(h * tok, tok)
        prod = g_st[rows, :].astype(jnp.float32) * o_st[rows, :].astype(jnp.float32)
        delta = jnp.sum(jnp.transpose(prod), axis=0, keepdims=True)
        rows_buf[0:1, rows] = delta * jnp.float32(1.0 / keep_scale)
        for r in range(4):
            active = (block_id - r >= 0) & (mask_smem[0, r] == 1)
            push = jnp.where(active, jnp.float32(0.0), jnp.float32(1e30))
            rows_buf[r + 1 : r + 2, rows] = norm_in[h : h + 1, :] + push

    def pass_on():
        for part in range(2):
            kv_wait(1, part)
            kv_copy(3, part, got_kv.at[0]).start()

    for part in range(2):
        kv_wait(2, part)

        @pl.when(parity == 1)
        def _():
            kv_copy(1, part, got_kv.at[1]).start()

    @pl.when(parity == 1)
    def _():
        pass_on()

    back_copies = {}
    for place, r in enumerate(OFFSETS):
        if r == 1:

            @pl.when(parity == 0)
            def _():
                pass_on()

        if r == 3:
            for part in range(2):
                kv_wait(3, part)
        if r > 0:
            key_blk = got_kv.at[r - 1, 0]
            value_blk = got_kv.at[r - 1, 1]
        else:
            key_blk = own_kv.at[0]
            value_blk = own_kv.at[1]
        s_buf[...] = dot(key_blk[...], q_st[...], NT)
        dp_buf[...] = dot(value_blk[...], g_st[...], NT)

        def pair_rows(i, carry, r=r):
            at = pl.ds(pl.multiple_of(i * ROWS, ROWS), ROWS)
            probs = jnp.exp(s_buf[at, :] * jnp.float32(scaling) - rows_buf[r + 1 : r + 2, :])
            if r == 0:
                probs = jnp.where(spread >= i * ROWS, probs, jnp.float32(0.0))
            if r == 3:
                probs = jnp.where(spread < i * ROWS + tok // 2, probs, jnp.float32(0.0))
            dropped = probs * kept[r, at, :]
            pk_buf[at, :] = dropped.astype(jnp.bfloat16)
            ds_buf[at, :] = (dropped * dp_buf[at, :] - probs * rows_buf[0:1, :]).astype(
                jnp.bfloat16
            )
            return carry

        for half, at in enumerate(halves):
            steps = half_rows // ROWS
            lax.fori_loop(half * steps, (half + 1) * steps, pair_rows, 0)
            add_key = dot(ds_buf[at, :], q_st[...], NN) * jnp.float32(keep_scale * scaling)
            add_value = dot(pk_buf[at, :], g_st[...], NN) * jnp.float32(keep_scale)
            if r > 0:
                back_out[r - 1, half, :, 0:hd] = add_key.astype(jnp.bfloat16)
                back_out[r - 1, half, :, hd : 2 * hd] = add_value.astype(jnp.bfloat16)
                copy = pltpu.make_async_remote_copy(
                    src_ref=back_out.at[r - 1, half],
                    dst_ref=back_in.at[r - 1, half],
                    send_sem=back_send.at[r - 1, half],
                    recv_sem=back_recv.at[r - 1, half],
                    device_id=(ctx_at(-r), group_id),
                    device_id_type=MESH,
                )
                copy.start()
                back_copies[r, half] = copy
            else:
                own_acc[at, 0:hd] = add_key
                own_acc[at, hd : 2 * hd] = add_value
        add_query = dot(key_blk[...], ds_buf[...], TN)
        if place == 0:
            dq_acc[...] = add_query
        else:
            dq_acc[...] += add_query

    for h in range(heads):
        part_t = jnp.transpose(dq_acc[:, pl.ds(h * tok, tok)])
        grads[:, pl.ds(h * hd, hd)] = (part_t * jnp.float32(keep_scale * scaling)).astype(
            jnp.bfloat16
        )

    for copy in weight_loads:
        copy.wait()

    def query_terms(i, carry):
        at = pl.ds(pl.multiple_of(i * tok, tok), tok)
        terms[i] = dot(grads[...], wq[at, :], NT)
        return carry

    lax.fori_loop(0, 16, query_terms, 0)

    def term(index, half):
        at = pl.ds(pl.multiple_of(index * tok, tok), tok)
        return terms[index, halves[half], :] + dot(kv_grads[halves[half], :], wkv[at, :], NT)

    pair_copies = {}

    def send_pair(j, half):
        value = term(chip_at(HOPS[j]) * 2 + 1 - core, half)
        pair_out[half, j] = value.astype(jnp.bfloat16)
        copy = pltpu.make_async_remote_copy(
            src_ref=pair_out.at[half, j],
            dst_ref=pair_in.at[half, j],
            send_sem=pair_send.at[half, j],
            recv_sem=pair_recv.at[half, j],
            device_id=(block_id, partner),
            device_id_type=MESH,
        )
        copy.start()
        pair_copies[j, half] = copy

    def far_copy(j, half):
        if j < 3:
            hop_y, hop_x = core * HOPS[j][0], 1 - core
        else:
            hop_y, hop_x = HOPS[j][0], HOPS[j][1]
        return pltpu.make_async_remote_copy(
            src_ref=far_out.at[half, j],
            dst_ref=far_in.at[half, j],
            send_sem=far_send.at[half, j],
            recv_sem=far_recv.at[half, j],
            device_id=(block_id, chip_at((hop_y, hop_x)) * 2 + core),
            device_id_type=MESH,
        )

    def send_far(j, half, value):
        far_out[half, j] = value.astype(jnp.bfloat16)
        far_copy(j, half).start()

    def first_phase(half):
        at = halves[half]
        for r in (2, 1, 3):
            back_copies[r, half].wait_recv()
        total = own_acc[at, :]
        for r in (1, 2, 3):
            total = total + back_in[r - 1, half].astype(jnp.float32)
        kv_grads[at, :] = total.astype(jnp.bfloat16)
        send_pair(0, half)
        send_pair(1, half)
        for j in range(8):
            if j + 2 < 8:
                send_pair(j + 2, half)
            own = term(chip_at(HOPS[j]) * 2 + core, half)
            pair_copies[j, half].wait_recv()
            own = own + pair_in[half, j].astype(jnp.float32)
            if j < 3:
                send_far(j, half, own)
            else:
                sums[j - 3, at, :] = own
            if 3 <= j < 7:

                @pl.when(core == (0 if j == 3 else 1))
                def _():
                    send_far(j, half, sums[j - 3, at, :])

    def second_phase(half):
        at = halves[half]

        @pl.when(core == 0)
        def _():
            for j in range(3):
                far_copy(j, half).wait_recv()
                value = sums[j + 1, at, :] + far_in[half, j].astype(jnp.float32)
                send_far(j + 4, half, value)

        @pl.when(core == 1)
        def _():
            total = sums[0, at, :]
            for j in range(3):
                far_copy(j, half).wait_recv()
                total = total + far_in[half, j].astype(jnp.float32)
            send_far(3, half, total)

    first_phase(0)
    first_phase(1)
    second_phase(0)
    second_phase(1)

    for half in range(2):
        for j in (4, 5, 6, 3):
            far_copy(j, half).wait_recv()

        def last_rows(i, carry, half=half):
            at = pl.ds(pl.multiple_of(i * ROWS, ROWS), ROWS)
            all_at = pl.ds(pl.multiple_of(i * ROWS + half * half_rows, ROWS), ROWS)
            total = sums[4, all_at, :]
            for j in range(3, 7):
                total = total + far_in[half, j, at, :].astype(jnp.float32)
            out_ref[all_at, :] = total
            return carry

        lax.fori_loop(0, half_rows // ROWS, last_rows, 0)

    sent = [kv_copy(r, part, own_kv) for r in (1, 2, 3) for part in range(2)]
    sent += list(back_copies.values()) + list(pair_copies.values())
    sent += [far_copy(j, half) for half in range(2) for j in range(7)]
    for copy in sent:
        copy.wait_send()


def on_device(*args):
    queries, keys, values, outputs, out_grad, log_norm = args[:6]
    q_weight = args[8]
    tok, hd = keys.shape
    heads = log_norm.shape[1]
    wide = heads * tok
    width = q_weight.shape[0]
    any_spec = pl.BlockSpec(memory_space=pl.ANY)
    smem_spec = pl.BlockSpec(memory_space=pltpu.SMEM)
    bf16, f32 = jnp.bfloat16, jnp.float32
    dma = pltpu.SemaphoreType.DMA
    operands = (queries, keys, values, outputs, out_grad, log_norm.T, *args[6:])
    held = [pltpu.with_memory_space_constraint(x, pltpu.HBM) for x in operands]
    total = pl.pallas_call(
        kernel,
        out_shape=jax.ShapeDtypeStruct((tok, width // 16), f32),
        in_specs=[any_spec] * 6 + [smem_spec] * 2 + [any_spec] * 3,
        out_specs=pl.BlockSpec(memory_space=pltpu.VMEM),
        scratch_shapes=[
            pltpu.VMEM((wide, hd), bf16),
            pltpu.VMEM((wide, hd), bf16),
            pltpu.VMEM((wide, hd), bf16),
            pltpu.VMEM((heads, tok), f32),
            pltpu.VMEM((2, tok, hd), bf16),
            pltpu.VMEM((3, 2, tok, hd), bf16),
            pltpu.VMEM((4, tok, wide), f32),
            pltpu.VMEM((tok, wide), f32),
            pltpu.VMEM((tok, wide), f32),
            pltpu.VMEM((tok, wide), bf16),
            pltpu.VMEM((tok, wide), bf16),
            pltpu.VMEM((8, wide), f32),
            pltpu.VMEM((hd, wide), f32),
            pltpu.VMEM((tok, 2 * hd), f32),
            pltpu.VMEM((3, 2, tok // 2, 2 * hd), bf16),
            pltpu.VMEM((3, 2, tok // 2, 2 * hd), bf16),
            pltpu.VMEM((tok, heads * hd), bf16),
            pltpu.VMEM((tok, 2 * hd), bf16),
            pltpu.VMEM((width, heads * hd), bf16),
            pltpu.VMEM((width, 2 * hd), bf16),
            pltpu.VMEM((16, tok, width // 16), f32),
            pltpu.VMEM((5, tok, width // 16), f32),
            pltpu.VMEM((2, 8, tok // 2, width // 16), bf16),
            pltpu.VMEM((2, 8, tok // 2, width // 16), bf16),
            pltpu.VMEM((2, 7, tok // 2, width // 16), bf16),
            pltpu.VMEM((2, 7, tok // 2, width // 16), bf16),
            dma((2 + 3 * heads + 1 + 3,)),
            dma((3, 2)),
            dma((3, 2)),
            dma((3, 2)),
            dma((3, 2)),
            dma((2, 8)),
            dma((2, 8)),
            dma((2, 7)),
            dma((2, 7)),
        ],
        compiler_params=pltpu.CompilerParams(
            collective_id=0,
            has_side_effects=True,
            vmem_limit_bytes=40 * 1024 * 1024,
        ),
    )(*held)
    return total.astype(bf16)


def solution(mesh):
    return jax.shard_map(
        on_device,
        mesh=mesh,
        in_specs=(
            P("ctx", "tp"),
            P("ctx", "tp"),
            P("ctx", "tp"),
            P("ctx", "tp"),
            P("ctx", "tp"),
            P("ctx", "tp"),
            P("ctx", None),
            P(),
            P(None, "tp"),
            P(None, "tp"),
            P(None, "tp"),
        ),
        out_specs=P("ctx", "tp"),
        check_vma=False,
    )
```

```python
import functools

import jax
import jax.numpy as jnp
from jax import lax
from jax.experimental import pallas as pl
from jax.experimental.pallas import tpu as pltpu
from jax.sharding import PartitionSpec as P

MESH = pl.DeviceIdType.MESH
keep_level = 103
keep_scale = 1024.0 / 921.0
ROWS = 16
NT = (((1,), (1,)), ((), ()))
NN = (((1,), (0,)), ((), ()))
TN = (((0,), (0,)), ((), ()))
HOPS = ((2, 1), (1, 1), (3, 1), (0, 1), (2, 0), (1, 0), (3, 0), (0, 0))
OFFSETS = (2, 1, 0, 3)


def dot(a, b, dims):
    return lax.dot_general(a, b, dims, preferred_element_type=jnp.float32)


def kernel(
    q_hbm,
    k_hbm,
    v_hbm,
    o_hbm,
    g_hbm,
    norm_hbm,
    mask_smem,
    base_smem,
    wq_hbm,
    wk_hbm,
    wv_hbm,
    out_ref,
    q_st,
    g_st,
    o_st,
    norm_in,
    own_kv,
    got_kv,
    kept,
    s_buf,
    dp_buf,
    pk_buf,
    ds_buf,
    rows_buf,
    dq_acc,
    own_acc,
    back_out,
    back_in,
    grads,
    kv_grads,
    wq,
    wkv,
    terms,
    sums,
    pair_out,
    pair_in,
    far_out,
    far_in,
    load_sem,
    kv_send,
    kv_recv,
    back_send,
    back_recv,
    pair_send,
    pair_recv,
    far_send,
    far_recv,
):
    tok = k_hbm.shape[0]
    hd = k_hbm.shape[1]
    heads = q_hbm.shape[1] // hd
    wide = heads * tok
    half_rows = tok // 2
    halves = [pl.ds(half * half_rows, half_rows) for half in range(2)]
    blocks = lax.axis_size("ctx")
    block_id = lax.axis_index("ctx")
    group_id = lax.axis_index("tp")
    y_pos = group_id // 4
    x_pos = (group_id // 2) % 2
    core = group_id % 2
    scaling = hd ** (-0.5)

    def ctx_at(steps):
        return lax.rem(block_id + steps + blocks, blocks)

    def at_least(steps):
        return block_id >= steps

    def room_for(steps):
        return block_id + steps < blocks

    def chip_at(hop):
        return lax.rem(y_pos + hop[0], 4) * 2 + lax.rem(x_pos + hop[1], 2)

    partner = group_id + 1 - 2 * core
    parity = block_id % 2
    x_peer = block_id + 1 - 2 * parity

    loads = []

    def load(src, dst):
        copy = pltpu.make_async_copy(src, dst, load_sem.at[len(loads)])
        copy.start()
        loads.append(copy)
        return copy

    kv_loads = [load(k_hbm, own_kv.at[0]), load(v_hbm, own_kv.at[1])]
    head_loads = []
    for src, dst in ((g_hbm, g_st), (o_hbm, o_st), (q_hbm, q_st)):
        for h in range(heads):
            head_loads.append(
                load(src.at[:, pl.ds(h * hd, hd)], dst.at[pl.ds(h * tok, tok), :])
            )
    norm_load = load(norm_hbm, norm_in)
    weight_loads = [
        load(wq_hbm, wq),
        load(wk_hbm, wkv.at[:, pl.ds(0, hd)]),
        load(wv_hbm, wkv.at[:, pl.ds(hd, hd)]),
    ]

    barrier = pltpu.get_barrier_semaphore()

    def greet(peer):
        pl.semaphore_signal(barrier, inc=1, device_id=peer, device_id_type=MESH)

    @pl.when(at_least(2))
    def _():
        greet((ctx_at(-2), group_id))

    @pl.when((parity == 1) | at_least(2))
    def _():
        greet((x_peer, group_id))

    greet((block_id, partner))
    for hop in HOPS[3:7]:
        greet((block_id, chip_at(hop) * 2 + core))
    to_far = jnp.where(room_for(2), 1, 0)
    to_near = jnp.where((parity == 0) | at_least(2), 1, 0)
    pl.semaphore_wait(barrier, 5 + to_far + to_near)

    for copy in kv_loads:
        copy.wait()
    def kv_copy(r, part, src):
        return pltpu.make_async_remote_copy(
            src_ref=src.at[part],
            dst_ref=got_kv.at[r - 1, part],
            send_sem=kv_send.at[r - 1, part],
            recv_sem=kv_recv.at[r - 1, part],
            device_id=(x_peer if r == 1 else ctx_at(2), group_id),
            device_id_type=MESH,
        )

    def kv_wait(r, part):
        kv_copy(r, part, own_kv).wait_recv()

    for part in range(2):

        @pl.when(room_for(2))
        def _():
            kv_copy(2, part, own_kv).start()

        @pl.when(parity == 0)
        def _():
            kv_copy(1, part, own_kv).start()

    lane = lax.broadcasted_iota(jnp.int32, (ROWS, wide), 1)
    sub = lax.broadcasted_iota(jnp.int32, (ROWS, wide), 0)
    head = lane // tok
    query = lane - head * tok
    spread = query - sub
    seed = base_smem[0]
    shift = base_smem[1]
    mixed_base = (
        (head + group_id * heads) * 83492791
        + query * 73856093
        + sub * 19349663
        + ((block_id * tok + shift) * 73856093 + seed)
    )

    def mask_rows(r):
        def step(i, carry):
            key_start = (block_id - r) * tok + i * ROWS + shift
            mixed = mixed_base + key_start * 19349663
            mixed = mixed ^ lax.shift_right_logical(mixed, jnp.int32(15))
            mixed = mixed * 739982445
            mixed = mixed ^ lax.shift_right_logical(mixed, jnp.int32(12))
            mixed = mixed * 695872825
            mixed = mixed ^ lax.shift_right_logical(mixed, jnp.int32(15))
            kept[r, pl.ds(pl.multiple_of(i * ROWS, ROWS), ROWS), :] = jnp.where(
                mixed & 1023 >= keep_level, jnp.float32(1.0), jnp.float32(0.0)
            )
            return carry

        lax.fori_loop(0, tok // ROWS, step, 0)

    for r in OFFSETS:
        mask_rows(r)

    for copy in head_loads:
        copy.wait()
    norm_load.wait()
    for h in range(heads):
        rows = pl.ds(h * tok, tok)
        prod = g_st[rows, :].astype(jnp.float32) * o_st[rows, :].astype(jnp.float32)
        delta = jnp.sum(jnp.transpose(prod), axis=0, keepdims=True)
        rows_buf[0:1, rows] = delta * jnp.float32(1.0 / keep_scale)
        for r in range(4):
            active = (block_id - r >= 0) & (mask_smem[0, r] == 1)
            push = jnp.where(active, jnp.float32(0.0), jnp.float32(1e30))
            rows_buf[r + 1 : r + 2, rows] = norm_in[h : h + 1, :] + push

    @pl.when((parity == 1) & at_least(2))
    def _():
        for part in range(2):
            kv_wait(2, part)
            kv_copy(1, part, got_kv.at[1]).start()

    @pl.when(at_least(1))
    def _():
        for part in range(2):
            kv_wait(1, part)

            @pl.when(room_for(2))
            def _():
                kv_copy(3, part, got_kv.at[0]).start()

    @pl.when((parity == 0) & at_least(2))
    def _():
        for part in range(2):
            kv_wait(2, part)

    def back_copy(r, half):
        return pltpu.make_async_remote_copy(
            src_ref=back_out.at[r - 1, half],
            dst_ref=back_in.at[r - 1, half],
            send_sem=back_send.at[r - 1, half],
            recv_sem=back_recv.at[r - 1, half],
            device_id=(ctx_at(-r), group_id),
            device_id_type=MESH,
        )

    def pair_grads(r):
        if r == 3:
            for part in range(2):
                kv_wait(3, part)
        if r > 0:
            key_blk = got_kv.at[r - 1, 0]
            value_blk = got_kv.at[r - 1, 1]
        else:
            key_blk = own_kv.at[0]
            value_blk = own_kv.at[1]
        s_buf[...] = dot(key_blk[...], q_st[...], NT)
        dp_buf[...] = dot(value_blk[...], g_st[...], NT)

        def pair_rows(i, carry, r=r):
            at = pl.ds(pl.multiple_of(i * ROWS, ROWS), ROWS)
            probs = jnp.exp(s_buf[at, :] * jnp.float32(scaling) - rows_buf[r + 1 : r + 2, :])
            if r == 0:
                probs = jnp.where(spread >= i * ROWS, probs, jnp.float32(0.0))
            if r == 3:
                probs = jnp.where(spread < i * ROWS + tok // 2, probs, jnp.float32(0.0))
            dropped = probs * kept[r, at, :]
            pk_buf[at, :] = dropped.astype(jnp.bfloat16)
            ds_buf[at, :] = (dropped * dp_buf[at, :] - probs * rows_buf[0:1, :]).astype(
                jnp.bfloat16
            )
            return carry

        for half, at in enumerate(halves):
            steps = half_rows // ROWS
            lax.fori_loop(half * steps, (half + 1) * steps, pair_rows, 0)
            add_key = dot(ds_buf[at, :], q_st[...], NN) * jnp.float32(keep_scale * scaling)
            add_value = dot(pk_buf[at, :], g_st[...], NN) * jnp.float32(keep_scale)
            if r > 0:
                back_out[r - 1, half, :, 0:hd] = add_key.astype(jnp.bfloat16)
                back_out[r - 1, half, :, hd : 2 * hd] = add_value.astype(jnp.bfloat16)
                back_copy(r, half).start()
            else:
                own_acc[at, 0:hd] = add_key
                own_acc[at, hd : 2 * hd] = add_value
        add_query = dot(key_blk[...], ds_buf[...], TN)
        dq_acc[...] += add_query

    dq_acc[...] = jnp.zeros_like(dq_acc)
    for r in OFFSETS:
        if r == 0:
            pair_grads(r)
        else:

            @pl.when(at_least(r))
            def _():
                pair_grads(r)

    for h in range(heads):
        part_t = jnp.transpose(dq_acc[:, pl.ds(h * tok, tok)])
        grads[:, pl.ds(h * hd, hd)] = (part_t * jnp.float32(keep_scale * scaling)).astype(
            jnp.bfloat16
        )

    for copy in weight_loads:
        copy.wait()

    def query_terms(i, carry):
        at = pl.ds(pl.multiple_of(i * tok, tok), tok)
        terms[i] = dot(grads[...], wq[at, :], NT)
        return carry

    lax.fori_loop(0, 16, query_terms, 0)

    def term(index, half):
        at = pl.ds(pl.multiple_of(index * tok, tok), tok)
        return terms[index, halves[half], :] + dot(kv_grads[halves[half], :], wkv[at, :], NT)

    pair_copies = {}

    def send_pair(j, half):
        value = term(chip_at(HOPS[j]) * 2 + 1 - core, half)
        pair_out[half, j] = value.astype(jnp.bfloat16)
        copy = pltpu.make_async_remote_copy(
            src_ref=pair_out.at[half, j],
            dst_ref=pair_in.at[half, j],
            send_sem=pair_send.at[half, j],
            recv_sem=pair_recv.at[half, j],
            device_id=(block_id, partner),
            device_id_type=MESH,
        )
        copy.start()
        pair_copies[j, half] = copy

    def far_copy(j, half):
        if j < 3:
            hop_y, hop_x = core * HOPS[j][0], 1 - core
        else:
            hop_y, hop_x = HOPS[j][0], HOPS[j][1]
        return pltpu.make_async_remote_copy(
            src_ref=far_out.at[half, j],
            dst_ref=far_in.at[half, j],
            send_sem=far_send.at[half, j],
            recv_sem=far_recv.at[half, j],
            device_id=(block_id, chip_at((hop_y, hop_x)) * 2 + core),
            device_id_type=MESH,
        )

    def send_far(j, half, value):
        far_out[half, j] = value.astype(jnp.bfloat16)
        far_copy(j, half).start()

    def first_phase(half):
        at = halves[half]
        for r in (2, 1, 3):

            @pl.when(room_for(r))
            def _():
                back_copy(r, half).wait_recv()
                own_acc[at, :] += back_in[r - 1, half].astype(jnp.float32)

        kv_grads[at, :] = own_acc[at, :].astype(jnp.bfloat16)
        send_pair(0, half)
        send_pair(1, half)
        for j in range(8):
            if j + 2 < 8:
                send_pair(j + 2, half)
            own = term(chip_at(HOPS[j]) * 2 + core, half)
            pair_copies[j, half].wait_recv()
            own = own + pair_in[half, j].astype(jnp.float32)
            if j < 3:
                send_far(j, half, own)
            else:
                sums[j - 3, at, :] = own
            if 3 <= j < 7:

                @pl.when(core == (0 if j == 3 else 1))
                def _():
                    send_far(j, half, sums[j - 3, at, :])

    def second_phase(half):
        at = halves[half]

        @pl.when(core == 0)
        def _():
            for j in range(3):
                far_copy(j, half).wait_recv()
                value = sums[j + 1, at, :] + far_in[half, j].astype(jnp.float32)
                send_far(j + 4, half, value)

        @pl.when(core == 1)
        def _():
            total = sums[0, at, :]
            for j in range(3):
                far_copy(j, half).wait_recv()
                total = total + far_in[half, j].astype(jnp.float32)
            send_far(3, half, total)

    first_phase(0)
    first_phase(1)
    second_phase(0)
    second_phase(1)

    for half in range(2):
        for j in (4, 5, 6, 3):
            far_copy(j, half).wait_recv()

        def last_rows(i, carry, half=half):
            at = pl.ds(pl.multiple_of(i * ROWS, ROWS), ROWS)
            all_at = pl.ds(pl.multiple_of(i * ROWS + half * half_rows, ROWS), ROWS)
            total = sums[4, all_at, :]
            for j in range(3, 7):
                total = total + far_in[half, j, at, :].astype(jnp.float32)
            out_ref[all_at, :] = total
            return carry

        lax.fori_loop(0, half_rows // ROWS, last_rows, 0)

    sends = (
        (room_for(2), [kv_copy(2, part, own_kv) for part in range(2)]),
        ((parity == 0) | at_least(2), [kv_copy(1, part, own_kv) for part in range(2)]),
        (at_least(1) & room_for(2), [kv_copy(3, part, own_kv) for part in range(2)]),
    )
    sends += tuple((at_least(r), [back_copy(r, half) for half in range(2)]) for r in (1, 2, 3))
    for sent, copies in sends:

        @pl.when(sent)
        def _():
            for copy in copies:
                copy.wait_send()

    for half in range(2):
        for j in range(8):
            pair_copies[j, half].wait_send()
        for j in range(7):
            far_copy(j, half).wait_send()


def on_device(*args):
    queries, keys, values, outputs, out_grad, log_norm = args[:6]
    q_weight = args[8]
    tok, hd = keys.shape
    heads = log_norm.shape[1]
    wide = heads * tok
    width = q_weight.shape[0]
    any_spec = pl.BlockSpec(memory_space=pl.ANY)
    smem_spec = pl.BlockSpec(memory_space=pltpu.SMEM)
    bf16, f32 = jnp.bfloat16, jnp.float32
    dma = pltpu.SemaphoreType.DMA
    operands = (queries, keys, values, outputs, out_grad, log_norm.T, *args[6:])
    held = [pltpu.with_memory_space_constraint(x, pltpu.HBM) for x in operands]
    total = pl.pallas_call(
        kernel,
        out_shape=jax.ShapeDtypeStruct((tok, width // 16), f32),
        in_specs=[any_spec] * 6 + [smem_spec] * 2 + [any_spec] * 3,
        out_specs=pl.BlockSpec(memory_space=pltpu.VMEM),
        scratch_shapes=[
            pltpu.VMEM((wide, hd), bf16),
            pltpu.VMEM((wide, hd), bf16),
            pltpu.VMEM((wide, hd), bf16),
            pltpu.VMEM((heads, tok), f32),
            pltpu.VMEM((2, tok, hd), bf16),
            pltpu.VMEM((3, 2, tok, hd), bf16),
            pltpu.VMEM((4, tok, wide), f32),
            pltpu.VMEM((tok, wide), f32),
            pltpu.VMEM((tok, wide), f32),
            pltpu.VMEM((tok, wide), bf16),
            pltpu.VMEM((tok, wide), bf16),
            pltpu.VMEM((8, wide), f32),
            pltpu.VMEM((hd, wide), f32),
            pltpu.VMEM((tok, 2 * hd), f32),
            pltpu.VMEM((3, 2, tok // 2, 2 * hd), bf16),
            pltpu.VMEM((3, 2, tok // 2, 2 * hd), bf16),
            pltpu.VMEM((tok, heads * hd), bf16),
            pltpu.VMEM((tok, 2 * hd), bf16),
            pltpu.VMEM((width, heads * hd), bf16),
            pltpu.VMEM((width, 2 * hd), bf16),
            pltpu.VMEM((16, tok, width // 16), f32),
            pltpu.VMEM((5, tok, width // 16), f32),
            pltpu.VMEM((2, 8, tok // 2, width // 16), bf16),
            pltpu.VMEM((2, 8, tok // 2, width // 16), bf16),
            pltpu.VMEM((2, 7, tok // 2, width // 16), bf16),
            pltpu.VMEM((2, 7, tok // 2, width // 16), bf16),
            dma((2 + 3 * heads + 1 + 3,)),
            dma((3, 2)),
            dma((3, 2)),
            dma((3, 2)),
            dma((3, 2)),
            dma((2, 8)),
            dma((2, 8)),
            dma((2, 7)),
            dma((2, 7)),
        ],
        compiler_params=pltpu.CompilerParams(
            collective_id=0,
            has_side_effects=True,
            vmem_limit_bytes=40 * 1024 * 1024,
        ),
    )(*held)
    return total.astype(bf16)


def solution(mesh):
    return jax.shard_map(
        on_device,
        mesh=mesh,
        in_specs=(
            P("ctx", "tp"),
            P("ctx", "tp"),
            P("ctx", "tp"),
            P("ctx", "tp"),
            P("ctx", "tp"),
            P("ctx", "tp"),
            P("ctx", None),
            P(),
            P(None, "tp"),
            P(None, "tp"),
            P(None, "tp"),
        ),
        out_specs=P("ctx", "tp"),
        check_vma=False,
    )
```

```python
import functools

import jax
import jax.numpy as jnp
from jax import lax
from jax.experimental import pallas as pl
from jax.experimental.pallas import tpu as pltpu
from jax.sharding import PartitionSpec as P

MESH = pl.DeviceIdType.MESH
keep_level = 103
keep_scale = 1024.0 / 921.0
ROWS = 16
NT = (((1,), (1,)), ((), ()))
NN = (((1,), (0,)), ((), ()))
TN = (((0,), (0,)), ((), ()))
HOPS = ((2, 1), (1, 1), (3, 1), (0, 1), (2, 0), (1, 0), (3, 0), (0, 0))
OFFSETS = (2, 1, 0, 3)


def dot(a, b, dims):
    return lax.dot_general(a, b, dims, preferred_element_type=jnp.float32)


def kernel(
    q_hbm,
    k_hbm,
    v_hbm,
    o_hbm,
    g_hbm,
    norm_hbm,
    mask_smem,
    base_smem,
    wq_hbm,
    wk_hbm,
    wv_hbm,
    out_ref,
    q_st,
    g_st,
    o_st,
    norm_in,
    own_kv,
    got_kv,
    kept,
    s_buf,
    dp_buf,
    pk_buf,
    ds_buf,
    rows_buf,
    dq_acc,
    own_acc,
    back_out,
    back_in,
    grads,
    kv_grads,
    wq,
    wkv,
    terms,
    sums,
    pair_out,
    pair_in,
    far_out,
    far_in,
    load_sem,
    kv_send,
    kv_recv,
    back_send,
    back_recv,
    pair_send,
    pair_recv,
    far_send,
    far_recv,
):
    tok = k_hbm.shape[0]
    hd = k_hbm.shape[1]
    heads = q_hbm.shape[1] // hd
    wide = heads * tok
    half_rows = tok // 2
    halves = [pl.ds(half * half_rows, half_rows) for half in range(2)]
    blocks = lax.axis_size("ctx")
    block_id = lax.axis_index("ctx")
    group_id = lax.axis_index("tp")
    y_pos = group_id // 4
    x_pos = (group_id // 2) % 2
    core = group_id % 2
    scaling = hd ** (-0.5)

    def ctx_at(steps):
        return lax.rem(block_id + steps + blocks, blocks)

    def at_least(steps):
        return block_id >= steps

    def room_for(steps):
        return block_id + steps < blocks

    def chip_at(hop):
        return lax.rem(y_pos + hop[0], 4) * 2 + lax.rem(x_pos + hop[1], 2)

    partner = group_id + 1 - 2 * core
    parity = block_id % 2
    x_peer = block_id + 1 - 2 * parity

    loads = []

    def load(src, dst):
        copy = pltpu.make_async_copy(src, dst, load_sem.at[len(loads)])
        copy.start()
        loads.append(copy)
        return copy

    kv_loads = [load(k_hbm, own_kv.at[0]), load(v_hbm, own_kv.at[1])]
    head_loads = []
    for src, dst in ((g_hbm, g_st), (o_hbm, o_st), (q_hbm, q_st)):
        for h in range(heads):
            head_loads.append(
                load(src.at[:, pl.ds(h * hd, hd)], dst.at[pl.ds(h * tok, tok), :])
            )
    norm_load = load(norm_hbm, norm_in)
    weight_loads = [
        load(wq_hbm, wq),
        load(wk_hbm, wkv.at[:, pl.ds(0, hd)]),
        load(wv_hbm, wkv.at[:, pl.ds(hd, hd)]),
    ]

    barrier = pltpu.get_barrier_semaphore()

    def greet(peer):
        pl.semaphore_signal(barrier, inc=1, device_id=peer, device_id_type=MESH)

    @pl.when(at_least(2))
    def _():
        greet((ctx_at(-2), group_id))

    @pl.when((parity == 1) | at_least(2))
    def _():
        greet((x_peer, group_id))

    greet((block_id, partner))
    for hop in HOPS[3:7]:
        greet((block_id, chip_at(hop) * 2 + core))
    to_far = jnp.where(room_for(2), 1, 0)
    to_near = jnp.where((parity == 0) | at_least(2), 1, 0)
    pl.semaphore_wait(barrier, 5 + to_far + to_near)

    for copy in kv_loads:
        copy.wait()
    def piece(part):
        return part // 2, halves[part % 2]

    def kv_copy(r, part, src):
        return pltpu.make_async_remote_copy(
            src_ref=src.at[piece(part)],
            dst_ref=got_kv.at[r - 1].at[piece(part)],
            send_sem=kv_send.at[r - 1, part],
            recv_sem=kv_recv.at[r - 1, part],
            device_id=(x_peer if r == 1 else ctx_at(2), group_id),
            device_id_type=MESH,
        )

    def kv_wait(r, part):
        kv_copy(r, part, own_kv).wait_recv()

    for part in range(4):

        @pl.when(room_for(2))
        def _():
            kv_copy(2, part, own_kv).start()

        @pl.when(parity == 0)
        def _():
            kv_copy(1, part, own_kv).start()

    lane = lax.broadcasted_iota(jnp.int32, (ROWS, wide), 1)
    sub = lax.broadcasted_iota(jnp.int32, (ROWS, wide), 0)
    head = lane // tok
    query = lane - head * tok
    spread = query - sub
    seed = base_smem[0]
    shift = base_smem[1]
    mixed_base = (
        (head + group_id * heads) * 83492791
        + query * 73856093
        + sub * 19349663
        + ((block_id * tok + shift) * 73856093 + seed)
    )

    def mask_rows(r):
        def step(i, carry):
            key_start = (block_id - r) * tok + i * ROWS + shift
            mixed = mixed_base + key_start * 19349663
            mixed = mixed ^ lax.shift_right_logical(mixed, jnp.int32(15))
            mixed = mixed * 739982445
            mixed = mixed ^ lax.shift_right_logical(mixed, jnp.int32(12))
            mixed = mixed * 695872825
            mixed = mixed ^ lax.shift_right_logical(mixed, jnp.int32(15))
            kept[r, pl.ds(pl.multiple_of(i * ROWS, ROWS), ROWS), :] = jnp.where(
                mixed & 1023 >= keep_level, jnp.float32(1.0), jnp.float32(0.0)
            )
            return carry

        lax.fori_loop(0, tok // ROWS, step, 0)

    for r in OFFSETS:
        mask_rows(r)

    def pass_on(part):
        kv_wait(1, part)

        @pl.when(room_for(2))
        def _():
            kv_copy(3, part, got_kv.at[0]).start()

    @pl.when(parity == 1)
    def _():
        for part in range(4):

            @pl.when(at_least(2))
            def _():
                kv_wait(2, part)
                kv_copy(1, part, got_kv.at[1]).start()

            pass_on(part)

    for copy in head_loads:
        copy.wait()
    norm_load.wait()
    for h in range(heads):
        rows = pl.ds(h * tok, tok)
        prod = g_st[rows, :].astype(jnp.float32) * o_st[rows, :].astype(jnp.float32)
        delta = jnp.sum(jnp.transpose(prod), axis=0, keepdims=True)
        rows_buf[0:1, rows] = delta * jnp.float32(1.0 / keep_scale)
        for r in range(4):
            active = (block_id - r >= 0) & (mask_smem[0, r] == 1)
            push = jnp.where(active, jnp.float32(0.0), jnp.float32(1e30))
            rows_buf[r + 1 : r + 2, rows] = norm_in[h : h + 1, :] + push

    def back_copy(r, half):
        return pltpu.make_async_remote_copy(
            src_ref=back_out.at[r - 1, half],
            dst_ref=back_in.at[r - 1, half],
            send_sem=back_send.at[r - 1, half],
            recv_sem=back_recv.at[r - 1, half],
            device_id=(ctx_at(-r), group_id),
            device_id_type=MESH,
        )

    def pair_grads(r):
        if r > 0:
            key_blk = got_kv.at[r - 1, 0]
            value_blk = got_kv.at[r - 1, 1]
        else:
            key_blk = own_kv.at[0]
            value_blk = own_kv.at[1]
        if r == 3:
            for part in range(2):
                kv_wait(3, part)
        s_buf[...] = dot(key_blk[...], q_st[...], NT)
        if r == 3:
            for part in range(2, 4):
                kv_wait(3, part)
        dp_buf[...] = dot(value_blk[...], g_st[...], NT)

        def pair_rows(i, carry, r=r):
            at = pl.ds(pl.multiple_of(i * ROWS, ROWS), ROWS)
            probs = jnp.exp(s_buf[at, :] * jnp.float32(scaling) - rows_buf[r + 1 : r + 2, :])
            if r == 0:
                probs = jnp.where(spread >= i * ROWS, probs, jnp.float32(0.0))
            if r == 3:
                probs = jnp.where(spread < i * ROWS + tok // 2, probs, jnp.float32(0.0))
            dropped = probs * kept[r, at, :]
            pk_buf[at, :] = dropped.astype(jnp.bfloat16)
            ds_buf[at, :] = (dropped * dp_buf[at, :] - probs * rows_buf[0:1, :]).astype(
                jnp.bfloat16
            )
            return carry

        for half, at in enumerate(halves):
            steps = half_rows // ROWS
            lax.fori_loop(half * steps, (half + 1) * steps, pair_rows, 0)
            add_key = dot(ds_buf[at, :], q_st[...], NN) * jnp.float32(keep_scale * scaling)
            add_value = dot(pk_buf[at, :], g_st[...], NN) * jnp.float32(keep_scale)
            if r > 0:
                back_out[r - 1, half, :, 0:hd] = add_key.astype(jnp.bfloat16)
                back_out[r - 1, half, :, hd : 2 * hd] = add_value.astype(jnp.bfloat16)
                back_copy(r, half).start()
            else:
                own_acc[at, 0:hd] = add_key
                own_acc[at, hd : 2 * hd] = add_value
        add_query = dot(key_blk[...], ds_buf[...], TN)
        dq_acc[...] += add_query

    dq_acc[...] = jnp.zeros_like(dq_acc)
    @pl.when(block_id == 2)
    def _():
        for part in range(4):
            pass_on(part)

    @pl.when((parity == 0) & at_least(2))
    def _():
        for part in range(4):
            kv_wait(2, part)

    for r in OFFSETS:
        if r == 1:

            @pl.when((parity == 0) & at_least(4))
            def _():
                for part in range(4):
                    pass_on(part)

        if r == 0:
            pair_grads(r)
        else:

            @pl.when(at_least(r))
            def _():
                pair_grads(r)

    for h in range(heads):
        part_t = jnp.transpose(dq_acc[:, pl.ds(h * tok, tok)])
        grads[:, pl.ds(h * hd, hd)] = (part_t * jnp.float32(keep_scale * scaling)).astype(
            jnp.bfloat16
        )

    for copy in weight_loads:
        copy.wait()

    def query_terms(i, carry):
        at = pl.ds(pl.multiple_of(i * tok, tok), tok)
        terms[i] = dot(grads[...], wq[at, :], NT)
        return carry

    lax.fori_loop(0, 16, query_terms, 0)

    def term(index, half):
        at = pl.ds(pl.multiple_of(index * tok, tok), tok)
        return terms[index, halves[half], :] + dot(kv_grads[halves[half], :], wkv[at, :], NT)

    pair_copies = {}

    def send_pair(j, half):
        value = term(chip_at(HOPS[j]) * 2 + 1 - core, half)
        pair_out[half, j] = value.astype(jnp.bfloat16)
        copy = pltpu.make_async_remote_copy(
            src_ref=pair_out.at[half, j],
            dst_ref=pair_in.at[half, j],
            send_sem=pair_send.at[half, j],
            recv_sem=pair_recv.at[half, j],
            device_id=(block_id, partner),
            device_id_type=MESH,
        )
        copy.start()
        pair_copies[j, half] = copy

    def far_copy(j, half):
        if j < 3:
            hop_y, hop_x = core * HOPS[j][0], 1 - core
        else:
            hop_y, hop_x = HOPS[j][0], HOPS[j][1]
        return pltpu.make_async_remote_copy(
            src_ref=far_out.at[half, j],
            dst_ref=far_in.at[half, j],
            send_sem=far_send.at[half, j],
            recv_sem=far_recv.at[half, j],
            device_id=(block_id, chip_at((hop_y, hop_x)) * 2 + core),
            device_id_type=MESH,
        )

    def send_far(j, half, value):
        far_out[half, j] = value.astype(jnp.bfloat16)
        far_copy(j, half).start()

    def first_phase(half):
        at = halves[half]
        for r in (2, 1, 3):

            @pl.when(room_for(r))
            def _():
                back_copy(r, half).wait_recv()
                own_acc[at, :] += back_in[r - 1, half].astype(jnp.float32)

        kv_grads[at, :] = own_acc[at, :].astype(jnp.bfloat16)
        send_pair(0, half)
        send_pair(1, half)
        for j in range(8):
            if j + 2 < 8:
                send_pair(j + 2, half)
            own = term(chip_at(HOPS[j]) * 2 + core, half)
            pair_copies[j, half].wait_recv()
            own = own + pair_in[half, j].astype(jnp.float32)
            if j < 3:
                send_far(j, half, own)
            else:
                sums[j - 3, at, :] = own
            if 3 <= j < 7:

                @pl.when(core == (0 if j == 3 else 1))
                def _():
                    send_far(j, half, sums[j - 3, at, :])

    def second_phase(half):
        at = halves[half]

        @pl.when(core == 0)
        def _():
            for j in range(3):
                far_copy(j, half).wait_recv()
                value = sums[j + 1, at, :] + far_in[half, j].astype(jnp.float32)
                send_far(j + 4, half, value)

        @pl.when(core == 1)
        def _():
            total = sums[0, at, :]
            for j in range(3):
                far_copy(j, half).wait_recv()
                total = total + far_in[half, j].astype(jnp.float32)
            send_far(3, half, total)

    first_phase(0)
    first_phase(1)
    second_phase(0)
    second_phase(1)

    for half in range(2):
        for j in (4, 5, 6, 3):
            far_copy(j, half).wait_recv()

        def last_rows(i, carry, half=half):
            at = pl.ds(pl.multiple_of(i * ROWS, ROWS), ROWS)
            all_at = pl.ds(pl.multiple_of(i * ROWS + half * half_rows, ROWS), ROWS)
            total = sums[4, all_at, :]
            for j in range(3, 7):
                total = total + far_in[half, j, at, :].astype(jnp.float32)
            out_ref[all_at, :] = total
            return carry

        lax.fori_loop(0, half_rows // ROWS, last_rows, 0)

    sends = (
        (room_for(2), [kv_copy(2, part, own_kv) for part in range(4)]),
        ((parity == 0) | at_least(2), [kv_copy(1, part, own_kv) for part in range(4)]),
        (at_least(1) & room_for(2), [kv_copy(3, part, own_kv) for part in range(4)]),
    )
    sends += tuple((at_least(r), [back_copy(r, half) for half in range(2)]) for r in (1, 2, 3))
    for sent, copies in sends:

        @pl.when(sent)
        def _():
            for copy in copies:
                copy.wait_send()

    for half in range(2):
        for j in range(8):
            pair_copies[j, half].wait_send()
        for j in range(7):
            far_copy(j, half).wait_send()


def on_device(*args):
    queries, keys, values, outputs, out_grad, log_norm = args[:6]
    q_weight = args[8]
    tok, hd = keys.shape
    heads = log_norm.shape[1]
    wide = heads * tok
    width = q_weight.shape[0]
    any_spec = pl.BlockSpec(memory_space=pl.ANY)
    smem_spec = pl.BlockSpec(memory_space=pltpu.SMEM)
    bf16, f32 = jnp.bfloat16, jnp.float32
    dma = pltpu.SemaphoreType.DMA
    operands = (queries, keys, values, outputs, out_grad, log_norm.T, *args[6:])
    held = [pltpu.with_memory_space_constraint(x, pltpu.HBM) for x in operands]
    total = pl.pallas_call(
        kernel,
        out_shape=jax.ShapeDtypeStruct((tok, width // 16), f32),
        in_specs=[any_spec] * 6 + [smem_spec] * 2 + [any_spec] * 3,
        out_specs=pl.BlockSpec(memory_space=pltpu.VMEM),
        scratch_shapes=[
            pltpu.VMEM((wide, hd), bf16),
            pltpu.VMEM((wide, hd), bf16),
            pltpu.VMEM((wide, hd), bf16),
            pltpu.VMEM((heads, tok), f32),
            pltpu.VMEM((2, tok, hd), bf16),
            pltpu.VMEM((3, 2, tok, hd), bf16),
            pltpu.VMEM((4, tok, wide), f32),
            pltpu.VMEM((tok, wide), f32),
            pltpu.VMEM((tok, wide), f32),
            pltpu.VMEM((tok, wide), bf16),
            pltpu.VMEM((tok, wide), bf16),
            pltpu.VMEM((8, wide), f32),
            pltpu.VMEM((hd, wide), f32),
            pltpu.VMEM((tok, 2 * hd), f32),
            pltpu.VMEM((3, 2, tok // 2, 2 * hd), bf16),
            pltpu.VMEM((3, 2, tok // 2, 2 * hd), bf16),
            pltpu.VMEM((tok, heads * hd), bf16),
            pltpu.VMEM((tok, 2 * hd), bf16),
            pltpu.VMEM((width, heads * hd), bf16),
            pltpu.VMEM((width, 2 * hd), bf16),
            pltpu.VMEM((16, tok, width // 16), f32),
            pltpu.VMEM((5, tok, width // 16), f32),
            pltpu.VMEM((2, 8, tok // 2, width // 16), bf16),
            pltpu.VMEM((2, 8, tok // 2, width // 16), bf16),
            pltpu.VMEM((2, 7, tok // 2, width // 16), bf16),
            pltpu.VMEM((2, 7, tok // 2, width // 16), bf16),
            dma((2 + 3 * heads + 1 + 3,)),
            dma((3, 4)),
            dma((3, 4)),
            dma((3, 2)),
            dma((3, 2)),
            dma((2, 8)),
            dma((2, 8)),
            dma((2, 7)),
            dma((2, 7)),
        ],
        compiler_params=pltpu.CompilerParams(
            collective_id=0,
            has_side_effects=True,
            vmem_limit_bytes=40 * 1024 * 1024,
        ),
    )(*held)
    return total.astype(bf16)


def solution(mesh):
    return jax.shard_map(
        on_device,
        mesh=mesh,
        in_specs=(
            P("ctx", "tp"),
            P("ctx", "tp"),
            P("ctx", "tp"),
            P("ctx", "tp"),
            P("ctx", "tp"),
            P("ctx", "tp"),
            P("ctx", None),
            P(),
            P(None, "tp"),
            P(None, "tp"),
            P(None, "tp"),
        ),
        out_specs=P("ctx", "tp"),
        check_vma=False,
    )
```

```python
import functools

import jax
import jax.numpy as jnp
from jax import lax
from jax.experimental import pallas as pl
from jax.experimental.pallas import tpu as pltpu
from jax.sharding import PartitionSpec as P

MESH = pl.DeviceIdType.MESH
keep_level = 103
keep_scale = 1024.0 / 921.0
ROWS = 16
NT = (((1,), (1,)), ((), ()))
NN = (((1,), (0,)), ((), ()))
TN = (((0,), (0,)), ((), ()))
HOPS = ((2, 1), (1, 1), (3, 1), (0, 1), (2, 0), (1, 0), (3, 0), (0, 0))
ORDER = ((2, 3, None), (1, 2, None), (0, 0, None), (3, 3, None), (2, 2, 2), (1, 1, 1))


def dot(a, b, dims):
    return lax.dot_general(a, b, dims, preferred_element_type=jnp.float32)


def kernel(
    q_hbm,
    k_hbm,
    v_hbm,
    o_hbm,
    g_hbm,
    norm_hbm,
    mask_hbm,
    base_hbm,
    wq_hbm,
    wk_hbm,
    wv_hbm,
    out_ref,
    q_st,
    g_st,
    o_st,
    norm_in,
    mask_smem,
    base_smem,
    own_kv,
    got_kv,
    kept,
    s_buf,
    dp_buf,
    pk_buf,
    ds_buf,
    rows_buf,
    dq_acc,
    own_acc,
    back_out,
    back_in,
    grads,
    kv_grads,
    wq,
    wkv,
    terms,
    sums,
    pair_out,
    pair_in,
    far_out,
    far_in,
    load_sem,
    kv_send,
    kv_recv,
    back_send,
    back_recv,
    pair_send,
    pair_recv,
    far_send,
    far_recv,
):
    tok = k_hbm.shape[0]
    hd = k_hbm.shape[1]
    heads = q_hbm.shape[1] // hd
    wide = heads * tok
    half_rows = tok // 2
    halves = [pl.ds(half * half_rows, half_rows) for half in range(2)]
    blocks = lax.axis_size("ctx")
    block_id = lax.axis_index("ctx")
    group_id = lax.axis_index("tp")
    y_pos = group_id // 4
    x_pos = (group_id // 2) % 2
    core = group_id % 2
    scaling = hd ** (-0.5)

    def ctx_at(steps):
        return lax.rem(block_id + steps + blocks, blocks)

    def at_least(steps):
        return block_id >= steps

    def room_for(steps):
        return block_id + steps < blocks

    def chip_at(hop):
        return lax.rem(y_pos + hop[0], 4) * 2 + lax.rem(x_pos + hop[1], 2)

    partner = group_id + 1 - 2 * core
    parity = block_id % 2
    x_peer = block_id + 1 - 2 * parity

    loads = []

    def load(src, dst):
        copy = pltpu.make_async_copy(src, dst, load_sem.at[len(loads)])
        copy.start()
        loads.append(copy)
        return copy

    small_loads = [load(mask_hbm, mask_smem), load(base_hbm, base_smem)]
    kv_loads = [load(k_hbm, own_kv.at[0]), load(v_hbm, own_kv.at[1])]
    head_loads = []
    for src, dst in ((g_hbm, g_st), (o_hbm, o_st), (q_hbm, q_st)):
        for h in range(heads):
            head_loads.append(
                load(src.at[:, pl.ds(h * hd, hd)], dst.at[pl.ds(h * tok, tok), :])
            )
    norm_load = load(norm_hbm, norm_in)
    weight_loads = [
        load(wq_hbm, wq),
        load(wk_hbm, wkv.at[:, pl.ds(0, hd)]),
        load(wv_hbm, wkv.at[:, pl.ds(hd, hd)]),
    ]

    barrier = pltpu.get_barrier_semaphore()

    def greet(peer):
        pl.semaphore_signal(barrier, inc=1, device_id=peer, device_id_type=MESH)

    @pl.when(at_least(2))
    def _():
        greet((ctx_at(-2), group_id))

    @pl.when((parity == 1) | at_least(2))
    def _():
        greet((x_peer, group_id))

    greet((block_id, partner))
    for hop in HOPS[3:7]:
        greet((block_id, chip_at(hop) * 2 + core))
    to_far = jnp.where(room_for(2), 1, 0)
    to_near = jnp.where((parity == 0) | at_least(2), 1, 0)
    pl.semaphore_wait(barrier, 5 + to_far + to_near)

    for copy in kv_loads:
        copy.wait()
    def piece(part):
        return part // 2, halves[part % 2]

    def kv_copy(r, part, src):
        return pltpu.make_async_remote_copy(
            src_ref=src.at[piece(part)],
            dst_ref=got_kv.at[r - 1].at[piece(part)],
            send_sem=kv_send.at[r - 1, part],
            recv_sem=kv_recv.at[r - 1, part],
            device_id=(x_peer if r == 1 else ctx_at(2), group_id),
            device_id_type=MESH,
        )

    def kv_wait(r, part):
        kv_copy(r, part, own_kv).wait_recv()

    for part in range(4):

        @pl.when(room_for(2))
        def _():
            kv_copy(2, part, own_kv).start()

        @pl.when(parity == 0)
        def _():
            kv_copy(1, part, own_kv).start()

    for copy in small_loads:
        copy.wait()

    lane = lax.broadcasted_iota(jnp.int32, (ROWS, wide), 1)
    sub = lax.broadcasted_iota(jnp.int32, (ROWS, wide), 0)
    head = lane // tok
    query = lane - head * tok
    spread = query - sub
    seed = base_smem[0]
    shift = base_smem[1]
    mixed_base = (
        (head + group_id * heads) * 83492791
        + query * 73856093
        + sub * 19349663
        + ((block_id * tok + shift) * 73856093 + seed)
    )

    def mask_rows(r):
        def step(i, carry):
            key_start = (block_id - r) * tok + i * ROWS + shift
            mixed = mixed_base + key_start * 19349663
            mixed = mixed ^ lax.shift_right_logical(mixed, jnp.int32(15))
            mixed = mixed * 739982445
            mixed = mixed ^ lax.shift_right_logical(mixed, jnp.int32(12))
            mixed = mixed * 695872825
            mixed = mixed ^ lax.shift_right_logical(mixed, jnp.int32(15))
            kept[r, pl.ds(pl.multiple_of(i * ROWS, ROWS), ROWS), :] = jnp.where(
                mixed & 1023 >= keep_level, jnp.float32(1.0), jnp.float32(0.0)
            )
            return carry

        lax.fori_loop(0, tok // ROWS, step, 0)

    for r in (2, 1, 0, 3):
        mask_rows(r)

    def pass_on(part):
        kv_wait(1, part)

        @pl.when(room_for(2))
        def _():
            kv_copy(3, part, got_kv.at[0]).start()

    @pl.when(parity == 1)
    def _():
        for part in range(4):

            @pl.when(at_least(2))
            def _():
                kv_wait(2, part)
                kv_copy(1, part, got_kv.at[1]).start()

            pass_on(part)

    for copy in head_loads:
        copy.wait()
    norm_load.wait()
    for h in range(heads):
        rows = pl.ds(h * tok, tok)
        prod = g_st[rows, :].astype(jnp.float32) * o_st[rows, :].astype(jnp.float32)
        delta = jnp.sum(jnp.transpose(prod), axis=0, keepdims=True)
        rows_buf[0:1, rows] = delta * jnp.float32(1.0 / keep_scale)
        for r in range(4):
            active = (block_id - r >= 0) & (mask_smem[0, r] == 1)
            push = jnp.where(active, jnp.float32(0.0), jnp.float32(1e30))
            rows_buf[r + 1 : r + 2, rows] = norm_in[h : h + 1, :] + push

    def back_copy(r, half):
        return pltpu.make_async_remote_copy(
            src_ref=back_out.at[r - 1, half],
            dst_ref=back_in.at[r - 1, half],
            send_sem=back_send.at[r - 1, half],
            recv_sem=back_recv.at[r - 1, half],
            device_id=(ctx_at(-r), group_id),
            device_id_type=MESH,
        )

    def pair_grads(r):
        if r > 0:
            key_blk = got_kv.at[r - 1, 0]
            value_blk = got_kv.at[r - 1, 1]
        else:
            key_blk = own_kv.at[0]
            value_blk = own_kv.at[1]
        if r == 3:
            for part in range(2):
                kv_wait(3, part)
        s_buf[...] = dot(key_blk[...], q_st[...], NT)
        if r == 3:
            for part in range(2, 4):
                kv_wait(3, part)
        dp_buf[...] = dot(value_blk[...], g_st[...], NT)

        def pair_rows(i, carry, r=r):
            at = pl.ds(pl.multiple_of(i * ROWS, ROWS), ROWS)
            probs = jnp.exp(s_buf[at, :] * jnp.float32(scaling) - rows_buf[r + 1 : r + 2, :])
            if r == 0:
                probs = jnp.where(spread >= i * ROWS, probs, jnp.float32(0.0))
            if r == 3:
                probs = jnp.where(spread < i * ROWS + tok // 2, probs, jnp.float32(0.0))
            dropped = probs * kept[r, at, :]
            pk_buf[at, :] = dropped.astype(jnp.bfloat16)
            ds_buf[at, :] = (dropped * dp_buf[at, :] - probs * rows_buf[0:1, :]).astype(
                jnp.bfloat16
            )
            return carry

        for half, at in enumerate(halves):
            steps = half_rows // ROWS
            lax.fori_loop(half * steps, (half + 1) * steps, pair_rows, 0)
            add_key = dot(ds_buf[at, :], q_st[...], NN) * jnp.float32(keep_scale * scaling)
            add_value = dot(pk_buf[at, :], g_st[...], NN) * jnp.float32(keep_scale)
            if r > 0:
                back_out[r - 1, half, :, 0:hd] = add_key.astype(jnp.bfloat16)
                back_out[r - 1, half, :, hd : 2 * hd] = add_value.astype(jnp.bfloat16)
                back_copy(r, half).start()
            else:
                own_acc[at, 0:hd] = add_key
                own_acc[at, hd : 2 * hd] = add_value
        add_query = dot(key_blk[...], ds_buf[...], TN)
        dq_acc[...] += add_query

    dq_acc[...] = jnp.zeros_like(dq_acc)
    @pl.when(block_id == 2)
    def _():
        for part in range(4):
            pass_on(part)

    @pl.when((parity == 0) & at_least(3))
    def _():
        for part in range(4):
            kv_wait(2, part)

    for r, first, last in ORDER:
        if r == 1 and last is None:

            @pl.when((parity == 0) & at_least(3))
            def _():
                for part in range(4):
                    pass_on(part)

        if r == 0:
            pair_grads(r)
        elif last is None:

            @pl.when(at_least(first))
            def _():
                pair_grads(r)

        else:

            @pl.when(block_id == first)
            def _():
                if r == 2:
                    for part in range(4):
                        kv_wait(2, part)
                pair_grads(r)

    for h in range(heads):
        part_t = jnp.transpose(dq_acc[:, pl.ds(h * tok, tok)])
        grads[:, pl.ds(h * hd, hd)] = (part_t * jnp.float32(keep_scale * scaling)).astype(
            jnp.bfloat16
        )

    for copy in weight_loads:
        copy.wait()

    def query_terms(i, carry):
        at = pl.ds(pl.multiple_of(i * tok, tok), tok)
        terms[i] = dot(grads[...], wq[at, :], NT)
        return carry

    lax.fori_loop(0, 16, query_terms, 0)

    def term(index, half):
        at = pl.ds(pl.multiple_of(index * tok, tok), tok)
        return terms[index, halves[half], :] + dot(kv_grads[halves[half], :], wkv[at, :], NT)

    pair_copies = {}

    def send_pair(j, half):
        value = term(chip_at(HOPS[j]) * 2 + 1 - core, half)
        pair_out[half, j] = value.astype(jnp.bfloat16)
        copy = pltpu.make_async_remote_copy(
            src_ref=pair_out.at[half, j],
            dst_ref=pair_in.at[half, j],
            send_sem=pair_send.at[half, j],
            recv_sem=pair_recv.at[half, j],
            device_id=(block_id, partner),
            device_id_type=MESH,
        )
        copy.start()
        pair_copies[j, half] = copy

    def y_first(half):
        return core if half == 0 else 1 - core

    def far_copy(j, half):
        if j < 3:
            hop_y, hop_x = y_first(half) * HOPS[j][0], 1 - y_first(half)
        else:
            hop_y, hop_x = HOPS[j][0], HOPS[j][1]
        return pltpu.make_async_remote_copy(
            src_ref=far_out.at[half, j],
            dst_ref=far_in.at[half, j],
            send_sem=far_send.at[half, j],
            recv_sem=far_recv.at[half, j],
            device_id=(block_id, chip_at((hop_y, hop_x)) * 2 + core),
            device_id_type=MESH,
        )

    def send_far(j, half, value):
        far_out[half, j] = value.astype(jnp.bfloat16)
        far_copy(j, half).start()

    def first_phase(half):
        at = halves[half]
        for r in (2, 1, 3):

            @pl.when(room_for(r))
            def _():
                back_copy(r, half).wait_recv()
                own_acc[at, :] += back_in[r - 1, half].astype(jnp.float32)

        kv_grads[at, :] = own_acc[at, :].astype(jnp.bfloat16)
        for j in range(8):
            send_pair(j, half)
        for j in range(8):
            own = term(chip_at(HOPS[j]) * 2 + core, half)
            pair_copies[j, half].wait_recv()
            own = own + pair_in[half, j].astype(jnp.float32)
            if j < 3:
                send_far(j, half, own)
            else:
                sums[j - 3, at, :] = own
            if 3 <= j < 7:

                @pl.when(y_first(half) == (0 if j == 3 else 1))
                def _():
                    send_far(j, half, sums[j - 3, at, :])

    def second_phase(half):
        at = halves[half]

        @pl.when(y_first(half) == 0)
        def _():
            for j in range(3):
                far_copy(j, half).wait_recv()
                value = sums[j + 1, at, :] + far_in[half, j].astype(jnp.float32)
                send_far(j + 4, half, value)

        @pl.when(y_first(half) == 1)
        def _():
            total = sums[0, at, :]
            for j in range(3):
                far_copy(j, half).wait_recv()
                total = total + far_in[half, j].astype(jnp.float32)
            send_far(3, half, total)

    first_phase(0)
    first_phase(1)
    second_phase(0)
    second_phase(1)

    for half in range(2):
        for j in (4, 5, 6, 3):
            far_copy(j, half).wait_recv()

        def last_rows(i, carry, half=half):
            at = pl.ds(pl.multiple_of(i * ROWS, ROWS), ROWS)
            all_at = pl.ds(pl.multiple_of(i * ROWS + half * half_rows, ROWS), ROWS)
            total = sums[4, all_at, :]
            for j in range(3, 7):
                total = total + far_in[half, j, at, :].astype(jnp.float32)
            out_ref[all_at, :] = total
            return carry

        lax.fori_loop(0, half_rows // ROWS, last_rows, 0)

    sends = (
        (room_for(2), [kv_copy(2, part, own_kv) for part in range(4)]),
        ((parity == 0) | at_least(2), [kv_copy(1, part, own_kv) for part in range(4)]),
        (at_least(1) & room_for(2), [kv_copy(3, part, own_kv) for part in range(4)]),
    )
    sends += tuple((at_least(r), [back_copy(r, half) for half in range(2)]) for r in (1, 2, 3))
    for sent, copies in sends:

        @pl.when(sent)
        def _():
            for copy in copies:
                copy.wait_send()

    for half in range(2):
        for j in range(8):
            pair_copies[j, half].wait_send()
        for j in range(7):
            far_copy(j, half).wait_send()


def on_device(*args):
    queries, keys, values, outputs, out_grad, log_norm = args[:6]
    q_weight = args[8]
    tok, hd = keys.shape
    heads = log_norm.shape[1]
    wide = heads * tok
    width = q_weight.shape[0]
    any_spec = pl.BlockSpec(memory_space=pl.ANY)
    bf16, f32 = jnp.bfloat16, jnp.float32
    dma = pltpu.SemaphoreType.DMA
    operands = (queries, keys, values, outputs, out_grad, log_norm.T, *args[6:])
    held = [pltpu.with_memory_space_constraint(x, pltpu.HBM) for x in operands]
    total = pl.pallas_call(
        kernel,
        out_shape=jax.ShapeDtypeStruct((tok, width // 16), f32),
        in_specs=[any_spec] * 11,
        out_specs=pl.BlockSpec(memory_space=pltpu.VMEM),
        scratch_shapes=[
            pltpu.VMEM((wide, hd), bf16),
            pltpu.VMEM((wide, hd), bf16),
            pltpu.VMEM((wide, hd), bf16),
            pltpu.VMEM((heads, tok), f32),
            pltpu.SMEM((1, 4), jnp.int32),
            pltpu.SMEM((2,), jnp.int32),
            pltpu.VMEM((2, tok, hd), bf16),
            pltpu.VMEM((3, 2, tok, hd), bf16),
            pltpu.VMEM((4, tok, wide), f32),
            pltpu.VMEM((tok, wide), f32),
            pltpu.VMEM((tok, wide), f32),
            pltpu.VMEM((tok, wide), bf16),
            pltpu.VMEM((tok, wide), bf16),
            pltpu.VMEM((8, wide), f32),
            pltpu.VMEM((hd, wide), f32),
            pltpu.VMEM((tok, 2 * hd), f32),
            pltpu.VMEM((3, 2, tok // 2, 2 * hd), bf16),
            pltpu.VMEM((3, 2, tok // 2, 2 * hd), bf16),
            pltpu.VMEM((tok, heads * hd), bf16),
            pltpu.VMEM((tok, 2 * hd), bf16),
            pltpu.VMEM((width, heads * hd), bf16),
            pltpu.VMEM((width, 2 * hd), bf16),
            pltpu.VMEM((16, tok, width // 16), f32),
            pltpu.VMEM((5, tok, width // 16), f32),
            pltpu.VMEM((2, 8, tok // 2, width // 16), bf16),
            pltpu.VMEM((2, 8, tok // 2, width // 16), bf16),
            pltpu.VMEM((2, 7, tok // 2, width // 16), bf16),
            pltpu.VMEM((2, 7, tok // 2, width // 16), bf16),
            dma((2 + 2 + 3 * heads + 1 + 3,)),
            dma((3, 4)),
            dma((3, 4)),
            dma((3, 2)),
            dma((3, 2)),
            dma((2, 8)),
            dma((2, 8)),
            dma((2, 7)),
            dma((2, 7)),
        ],
        compiler_params=pltpu.CompilerParams(
            collective_id=0,
            has_side_effects=True,
            vmem_limit_bytes=40 * 1024 * 1024,
        ),
    )(*held)
    return total.astype(bf16)


def solution(mesh):
    return jax.shard_map(
        on_device,
        mesh=mesh,
        in_specs=(
            P("ctx", "tp"),
            P("ctx", "tp"),
            P("ctx", "tp"),
            P("ctx", "tp"),
            P("ctx", "tp"),
            P("ctx", "tp"),
            P("ctx", None),
            P(),
            P(None, "tp"),
            P(None, "tp"),
            P(None, "tp"),
        ),
        out_specs=P("ctx", "tp"),
        check_vma=False,
    )
```
